32 devices in a mesh: party: 2 (over x), dp: 16 (over z, y, core).
Axes of the slice: x: 2, y: 2, z: 4, core: 2. Of those that a mesh axis runs over, the one named last changes fastest.
Arguments:
- x_share: float32 [2, 8192, 1024], P('party', 'dp'), may hold values from -6 to 6
- w_share: float32 [2, 1024, 2048], P('party', 'dp'), may hold values from -0.1875 to 0.1875
- g_share: float32 [2, 8192, 2048], P('party', 'dp'), may hold values from -0.0625 to 0.0625
- fwd_a: float32 [2, 8192, 1024], P('party', 'dp'), may hold values from -4 to 4
- fwd_b: float32 [2, 1024, 2048], P('party', 'dp'), may hold values from -0.125 to 0.125
- fwd_c: float32 [2, 8192, 2048], P('party', 'dp'), may hold values from -2100 to 2100, as said below
- bwd_a: float32 [2, 8192, 1024], P('party', 'dp'), may hold values from -4 to 4
- bwd_b: float32 [2, 8192, 2048], P('party', 'dp'), may hold values from -0.044194174 to 0.044194174
- bwd_c: float32 [2, 1024, 2048], P('party', 'dp'), may hold values from -2100 to 2100, as said below
Outputs:
- y_share: float32 [2, 8192, 2048], P('party', 'dp')
- dw_share: float32 [2, 1024, 2048], P('party', 'dp')
The draws below stay inside these ranges and needn't reach their ends.
Inputs may be any that keep to these rules, and one draw needn't show every extreme that they name: fwd_c[0] + fwd_c[1] equals (fwd_a[0] + fwd_a[1]) (fwd_b[0] + fwd_b[1]) up to float32 rounding. bwd_c[0] + bwd_c[1] equals (bwd_a[0] + bwd_a[1])^T (bwd_b[0] + bwd_b[1]) up to float32 rounding.
All inputs are finite; a program needn't handle non-finite values.
Results may differ from the reference program's by a relative error of at most 0.0001.
Values sent between devices are 32-bit elements; how exact they have to be, the bound alone decides.
A program may use at most 128 MiB of HBM per device.

```python
import jax
import jax.numpy as jnp
from jax import lax

D = 1024
FF = 2048
TOKENS = 8192


def factor_left(key, salt):
    return jnp.clip(jax.random.normal(jax.random.fold_in(key, salt), (2, TOKENS, D), jnp.float32), -4.0, 4.0)


def forward_right(key):
    values = jnp.clip(jax.random.normal(jax.random.fold_in(key, 21), (2, D, FF), jnp.float32), -4.0, 4.0)
    return values * (1.0 / 32.0)


def backward_right(key):
    values = jnp.clip(jax.random.normal(jax.random.fold_in(key, 31), (2, TOKENS, FF), jnp.float32), -4.0, 4.0)
    return values * (1.0 / TOKENS) ** 0.5


def draw_fwd_a(key, part):
    return factor_left(key, 11)


def draw_fwd_b(key, part):
    return forward_right(key)


def draw_fwd_c(key, part):
    left = factor_left(key, 11)
    right = forward_right(key)
    product = jnp.dot(left[0] + left[1], right[0] + right[1], precision=lax.Precision.HIGHEST, preferred_element_type=jnp.float32)
    masking = jnp.clip(jax.random.normal(jax.random.fold_in(key, 41), (TOKENS, FF), jnp.float32), -4.0, 4.0)
    return jnp.stack([product - masking, masking])


def draw_bwd_a(key, part):
    return factor_left(key, 13)


def draw_bwd_b(key, part):
    return backward_right(key)


def draw_bwd_c(key, part):
    left = factor_left(key, 13)
    right = backward_right(key)
    product = lax.dot_general(left[0] + left[1], right[0] + right[1], (((0,), (0,)), ((), ())), precision=lax.Precision.HIGHEST, preferred_element_type=jnp.float32)
    masking = jnp.clip(jax.random.normal(jax.random.fold_in(key, 43), (D, FF), jnp.float32), -4.0, 4.0)
    return jnp.stack([product - masking, masking])


def steps_of(rng, dims, cuts, smallest, largest):
    level = 1.0
    for dim, parts in cuts:
        draws = jax.random.uniform(jax.random.fold_in(jax.random.fold_in(rng, 6), dim), (parts,), jnp.float32, smallest / len(cuts), largest / len(cuts))
        level = level * jnp.repeat(jnp.exp(draws), dims[dim] // parts).reshape((-1,) + (1,) * (len(dims) - 1 - dim))
    return level


def noise(stream_key, extent, scale, limit, shards=(), held_as=jnp.bfloat16):
    level = steps_of(stream_key, extent, shards, -0.22, 0.18) if shards else 1.0
    drawn = jax.random.normal(stream_key, extent, jnp.float32) * scale * level
    return jnp.minimum(jnp.maximum(drawn, -limit), limit).astype(held_as)


def setup_inputs(seed: int = 0) -> dict:
    key_of = jax.random.split(jax.random.key(seed), 10)
    return {
        "x_share": noise(key_of[0], (2, TOKENS, D), 1.0, 6.0, ((0, 2), (1, 16)), jnp.float32),
        "w_share": noise(key_of[1], (2, D, FF), D ** -0.5, 0.1875, ((0, 2), (1, 16)), jnp.float32),
        "g_share": noise(key_of[2], (2, TOKENS, FF), TOKENS ** -0.5, 0.0625, ((0, 2), (1, 16)), jnp.float32),
        "fwd_a": draw_fwd_a(jax.random.fold_in(key_of[9], 71), 0),
        "fwd_b": draw_fwd_b(jax.random.fold_in(key_of[9], 71), 0),
        "fwd_c": draw_fwd_c(jax.random.fold_in(key_of[9], 71), 0),
        "bwd_a": draw_bwd_a(jax.random.fold_in(key_of[9], 71), 0),
        "bwd_b": draw_bwd_b(jax.random.fold_in(key_of[9], 71), 0),
        "bwd_c": draw_bwd_c(jax.random.fold_in(key_of[9], 71), 0),
    }


def matmul(left, right):
    return jnp.dot(left, right, preferred_element_type=jnp.float32, precision=lax.Precision.HIGHEST)


def tmatmul(left, right):
    return lax.dot_general(left, right, (((0,), (0,)), ((), ())), precision=lax.Precision.HIGHEST, preferred_element_type=jnp.float32)


def reference(x_share, w_share, g_share, fwd_a, fwd_b, fwd_c, bwd_a, bwd_b, bwd_c):
    eps_fwd = (x_share[0] - fwd_a[0]) + (x_share[1] - fwd_a[1])
    delta_fwd = (w_share[0] - fwd_b[0]) + (w_share[1] - fwd_b[1])
    eps_bwd = (x_share[0] - bwd_a[0]) + (x_share[1] - bwd_a[1])
    delta_bwd = (g_share[0] - bwd_b[0]) + (g_share[1] - bwd_b[1])
    outputs = []
    grads = []
    for party in range(2):
        first = jnp.float32(1.0 if party == 0 else 0.0)
        outputs.append(fwd_c[party] + matmul(eps_fwd, fwd_b[party] + first * delta_fwd) + matmul(fwd_a[party], delta_fwd))
        grads.append(bwd_c[party] + tmatmul(eps_bwd, bwd_b[party] + first * delta_bwd) + tmatmul(bwd_a[party], delta_bwd))
    return jnp.stack(outputs), jnp.stack(grads)
```

```python
import functools

import jax
import jax.numpy as jnp
from jax import lax
from jax.experimental import pallas as pl
from jax.experimental.pallas import tpu as pltpu
from jax.sharding import PartitionSpec as P

MESH = pl.DeviceIdType.MESH
BF16, F32 = jnp.bfloat16, jnp.float32
SUBS = 2
LAG = 2
TILE = 256
WIDE = 512


def position(chip, nc):
    z, y = chip // 2, lax.rem(chip, 2)
    return z + y * (nc - 1 - 2 * z)


def chip_at(spot, nc):
    spot = lax.rem(spot + 2 * nc, nc)
    y = spot // (nc // 2)
    z = spot + y * (nc - 1 - 2 * spot)
    return 2 * z + y


def split(value):
    high = value.astype(BF16)
    return high, (value - high.astype(F32)).astype(BF16)


def product(left, right):
    def dot(a, b):
        return jnp.dot(a, b, preferred_element_type=F32)

    return dot(left[0], right[0]) + (dot(left[1], right[0]) + dot(left[0], right[1]))


def kernel(
    n,
    x_ref,
    g_ref,
    fa_ref,
    fc_ref,
    ba_ref,
    bb_ref,
    w_ref,
    fb_ref,
    bc_ref,
    y_ref,
    dw_ref,
    wts,
    rx,
    ra,
    rg,
    uo,
    ru,
    acc,
    mate,
    slots,
    lefts,
    right,
    sx,
    sx2,
    sa,
    sa2,
    sg,
    sb,
    sg2,
    tiles,
    ybuf,
    own_w,
    got_w,
    delta,
    give,
    got,
    ld_sem,
    tile_sem,
    y_sem,
    lc_sem,
    xs_send,
    xs_recv,
    sw_send,
    sw_recv,
    ag_send,
    ag_recv,
    ac_send,
    ac_recv,
    rs_send,
    rs_recv,
    mt_send,
    mt_recv,
):
    nc = n // 2
    steps = nc - 1
    party, me = lax.axis_index("party"), lax.axis_index("dp")
    core, chip = lax.rem(me, 2), me // 2
    spot = position(chip, nc)
    rows, ff = fb_ref.shape
    tokens, d = x_ref.shape
    quarter, eighth = tokens // 4, tokens // 8
    piece = ff // (2 * SUBS)
    first = party == 0
    other = {"party": 1 - party}
    buddy = {"dp": me + 1 - 2 * core}
    ahead = {"dp": 2 * chip_at(spot + 1, nc) + core}
    behind = {"dp": 2 * chip_at(spot - 1, nc) + core}

    def cols_of(way, sub):
        return pl.ds((way * SUBS + sub) * piece, piece)

    def half_of(way):
        return pl.ds(way * (ff // 2), ff // 2)

    def remote(src, dst, send, recv, device):
        return pltpu.make_async_remote_copy(
            src_ref=src, dst_ref=dst, send_sem=send, recv_sem=recv, device_id=device, device_id_type=MESH
        )

    own_w[...] = w_ref[...] - fb_ref[...]
    barrier = pltpu.get_barrier_semaphore()
    for device in (other, buddy, ahead, behind):
        pl.semaphore_signal(barrier, inc=1, device_id=device, device_id_type=MESH)
    pl.semaphore_wait(barrier, 4)

    def chunk_copies(side, j):
        start = j * 2 * quarter
        k = 1 + 2 * j
        if side == 0:
            everything = pl.ds(start, 2 * quarter)
            tail = pl.ds(start + 3 * eighth, eighth)
            return [
                remote(x_ref.at[everything], rx.at[everything], xs_send.at[k], xs_recv.at[k], other),
                remote(g_ref.at[tail], rg.at[pl.ds(j * eighth, eighth)], xs_send.at[k + 1], xs_recv.at[k + 1], other),
            ]
        head = pl.ds(start, 3 * eighth)
        return [
            remote(x_ref.at[head], rx.at[head], xs_send.at[k], xs_recv.at[k], other),
            remote(ba_ref.at[head], ra.at[head], xs_send.at[k + 1], xs_recv.at[k + 1], other),
        ]

    def mask_copy():
        return remote(own_w, got_w, xs_send.at[0], xs_recv.at[0], other)

    def open_copy():
        return remote(uo, ru, xs_send.at[5], xs_recv.at[5], other)

    def gather_copy(m, way, sub, step):
        owner = chip_at(spot - step, nc) if way == 0 else chip_at(spot + step, nc)
        return remote(
            wts.at[m, owner, core, :, cols_of(way, sub)],
            wts.at[m, owner, core, :, cols_of(way, sub)],
            ag_send.at[m, way, sub, step],
            ag_recv.at[m, way, sub, step],
            ahead if way == 0 else behind,
        )

    def gather_first(m, way, sub, source):
        return remote(
            source.at[:, cols_of(way, sub)],
            wts.at[m, chip, core, :, cols_of(way, sub)],
            ag_send.at[m, way, sub, 0],
            ag_recv.at[m, way, sub, 0],
            ahead if way == 0 else behind,
        )

    def gather_arrival(m, way, sub, step):
        owner = chip_at(spot - 1 - step, nc) if way == 0 else chip_at(spot + 1 + step, nc)
        here = wts.at[m, owner, core, :, cols_of(way, sub)]
        return remote(here, here, ag_send.at[m, way, sub, step], ag_recv.at[m, way, sub, step], ahead)

    def begin_gather(m, source):
        for sub in range(SUBS):
            for way in range(2):
                gather_first(m, way, sub, source).start()
        remote(source, wts.at[m, chip, core], ac_send.at[m], ac_recv.at[m], buddy).start()
        pltpu.make_async_copy(source, wts.at[m, chip, core], lc_sem.at[m]).start()

    def pass_on(m, step):
        for sub in range(SUBS):
            for way in range(2):
                gather_arrival(m, way, sub, step).wait_recv()

                @pl.when(step < steps - 1)
                def _():
                    gather_copy(m, way, sub, step + 1).start()

        for way in range(2):
            owner = chip_at(spot - 1 - step, nc) if way == 0 else chip_at(spot + 1 + step, nc)
            here = wts.at[m, owner, core, :, half_of(way)]
            remote(here, here, ac_send.at[m], ac_recv.at[m], buddy).start()

    def load(src, dst, k):
        return pltpu.make_async_copy(src, dst, ld_sem.at[k])

    def open_rows(i):
        part = pl.ds(pl.multiple_of(i * quarter, 8), quarter)
        copies = [load(x_ref.at[part], sx, 0), load(fa_ref.at[part], sa, 1)]
        for copy in copies:
            copy.start()
        for copy in copies:
            copy.wait()
        sx2[...] = sx[...] - sa[...]
        out = load(sx2, uo.at[part], 2)
        out.start()
        out.wait()

    def put_left(k, at, value):
        high, low = split(value)
        lefts[k, 0, :, at] = high.T
        lefts[k, 1, :, at] = low.T

    def put_right(k, at, value):
        high, low = split(value)
        for half in range(2):
            to = slice(half * 2 * quarter + at.start, half * 2 * quarter + at.stop)
            right[2 * k, to, :] = high[:, half * (ff // 2) : (half + 1) * (ff // 2)]
            right[2 * k + 1, to, :] = low[:, half * (ff // 2) : (half + 1) * (ff // 2)]

    def operands(j):
        for part in range(2):
            start = (2 * j + part) * quarter
            here = pl.ds(start, quarter)
            to = slice(part * quarter, (part + 1) * quarter)
            own = [
                load(x_ref.at[here], sx, 0),
                load(ba_ref.at[here], sa, 1),
                load(g_ref.at[here], sg, 2),
                load(bb_ref.at[here], sb, 3),
            ]
            for copy in own:
                copy.start()

            @pl.when(first)
            def _():
                if part == 0:
                    for copy in chunk_copies(1, j):
                        copy.wait_recv()
                many = quarter if part == 0 else eighth
                some = pl.ds(start, many)
                more = [load(rx.at[some], sx2.at[pl.ds(0, many)], 4), load(ra.at[some], sa2.at[pl.ds(0, many)], 5)]
                for copy in more:
                    copy.start()
                for copy in own + more:
                    copy.wait()
                if part == 1:
                    sx2[many:, :] = jnp.zeros((quarter - many, d), F32)
                    sa2[many:, :] = jnp.zeros((quarter - many, d), F32)
                    sx[many:, :] = jnp.zeros((quarter - many, d), F32)
                    sg[many:, :] = jnp.zeros((quarter - many, ff), F32)
                put_left(0, to, sa2[...])
                put_left(1, to, (sx[...] + sx2[...]) - sa2[...])
                put_left(2, to, sa[...])
                put_right(0, to, sg[...])
                put_right(1, to, sb[...])

            @pl.when(jnp.logical_not(first))
            def _():
                if part == 0:
                    for copy in chunk_copies(0, j):
                        copy.wait_recv()
                more = [load(rx.at[here], sx2, 4)]
                if part == 1:
                    more.append(load(rg.at[pl.ds(j * eighth, eighth)], sg2, 5))
                for copy in more:
                    copy.start()
                for copy in own + more:
                    copy.wait()
                sg[...] = sg[...] - sb[...]
                if part == 1:
                    sg[eighth:, :] = sg[eighth:, :] + sg2[...]
                opened = sx[...] + sx2[...]
                put_left(0, to, opened - sa[...])
                put_left(1, to, sa[...])
                put_left(2, to, opened)
                put_right(0, to, sg[...])
                put_right(1, to, sb[...])

    keep = jnp.where(first, 1.0, 0.0).astype(F32)
    sign = 1.0 - 2.0 * keep
    group = d // 4
    per = group // (2 * rows)

    def gradient_rows(j, q):
        at = pl.ds(pl.multiple_of(q * group, group), group)
        chips = pl.ds(q * per, per)

        def tile(t, carry):
            half = t // (ff // 2 // WIDE)
            deep = pl.ds(pl.multiple_of(half * 2 * quarter, 2 * quarter), 2 * quarter)
            wide = pl.ds(pl.multiple_of(lax.rem(t, ff // 2 // WIDE) * WIDE, WIDE), WIDE)
            cols = pl.ds(pl.multiple_of(t * WIDE, WIDE), WIDE)

            def multiply(k, m):
                return product(
                    (lefts[k, 0, at, :], lefts[k, 1, at, :]),
                    (right[2 * m, deep, wide], right[2 * m + 1, deep, wide]),
                )

            shared = multiply(2, 1)
            shape = (per, 2, rows, WIDE)
            foreign = (multiply(0, 0) + keep * shared).reshape(shape)
            mine = (multiply(1, 0) + sign * shared).reshape(shape)
            if j == 0:
                acc[0, chips, :, :, cols] = foreign
                acc[1, chips, :, :, cols] = mine
            else:
                acc[0, chips, :, :, cols] = acc[0, chips, :, :, cols] + foreign
                acc[1, chips, :, :, cols] = acc[1, chips, :, :, cols] + mine
            return carry

        lax.fori_loop(0, ff // WIDE, tile, 0)

    begin_gather(0, fb_ref)
    mask_copy().start()
    for side in range(2):

        @pl.when(party == side)
        def _():
            for j in range(2):
                for copy in chunk_copies(side, j):
                    copy.start()

    early = steps - 3

    def gather_step(i, carry):
        @pl.when(i < steps)
        def _():
            pass_on(0, i)

        @pl.when(i < 4)
        def _():
            open_rows(i)

        @pl.when(i == 3)
        def _():
            open_copy().start()

        @pl.when(i == early)
        def _():
            operands(0)

        @pl.when(i > early)
        def _():
            @pl.when(i <= early + 2)
            def _():
                gradient_rows(0, 2 * (i - early - 1))

        @pl.when(i == LAG - 1)
        def _():
            mask_copy().wait_recv()
            delta[...] = own_w[...] + got_w[...]
            begin_gather(1, delta)

        @pl.when(i >= LAG)
        def _():
            pass_on(1, i - LAG)

        @pl.when(i > early)
        def _():
            @pl.when(i <= early + 2)
            def _():
                gradient_rows(0, 2 * (i - early - 1) + 1)

        return carry

    lax.fori_loop(0, steps + LAG, gather_step, 0)

    operands(1)

    def second(q, carry):
        gradient_rows(1, q)
        return carry

    lax.fori_loop(0, 4, second, 0)

    def mate_copy(m, to_chip):
        return remote(acc.at[m, to_chip, 1 - core], mate.at[m, to_chip], mt_send.at[m], mt_recv.at[m, to_chip], buddy)

    def mate_pair(k, carry):
        for m in range(2):
            mate_copy(m, chip_at(spot - k, nc)).start()
            mate_copy(m, chip_at(spot + k, nc)).start()
        return carry

    lax.fori_loop(1, nc // 2, mate_pair, 0)
    for m in range(2):
        mate_copy(m, chip_at(spot + nc // 2, nc)).start()
    for m in range(2):
        mate_copy(m, chip).start()
    fetch_y = load(fc_ref, ybuf, 6)
    fetch_y.start()
    for m in range(2):
        pltpu.make_async_copy(wts.at[m, chip, core], wts.at[m, chip, core], lc_sem.at[m]).wait()
        everything = remote(wts.at[m, :, core], wts.at[m, :, 1 - core], ac_send.at[m], ac_recv.at[m], buddy)
        everything.wait_recv()
        everything.wait_send()

    def owner_of(way, step):
        return chip_at(spot - 1 - step, nc) if way == 0 else chip_at(spot + 1 + step, nc)

    def sum_copy(m, way, sub, step, source):
        return remote(
            source,
            slots.at[m, way, sub, step],
            rs_send.at[m, way, sub, step],
            rs_recv.at[m, way, sub, step],
            ahead if way == 0 else behind,
        )

    def mate_arrivals(m, step):
        mate_copy(m, owner_of(0, step)).wait_recv()

        @pl.when(step < nc // 2 - 1)
        def _():
            mate_copy(m, owner_of(1, step)).wait_recv()

    def sum_start(m):
        mate_arrivals(m, 0)
        for sub in range(SUBS):
            for way in range(2):
                owner, cols = owner_of(way, 0), cols_of(way, sub)
                acc[m, owner, core, :, cols] = acc[m, owner, core, :, cols] + mate[m, owner, :, cols]
                sum_copy(m, way, sub, 0, acc.at[m, owner, core, :, cols]).start()

    def sum_step(m, step):
        @pl.when(step < nc // 2)
        def _():
            mate_arrivals(m, step)

        for sub in range(SUBS):
            for way in range(2):
                owner, cols = owner_of(way, step), cols_of(way, sub)
                held = slots.at[m, way, sub, step - 1]
                sum_copy(m, way, sub, step - 1, held).wait_recv()
                slots[m, way, sub, step - 1] = slots[m, way, sub, step - 1] + (
                    acc[m, owner, core, :, cols] + mate[m, owner, :, cols]
                )
                sum_copy(m, way, sub, step, held).start()

    nt = ff // TILE

    def fetch(m, t, buf):
        cols = pl.ds(pl.multiple_of(t * TILE, TILE), TILE)
        return pltpu.make_async_copy(wts.at[m, :, :, :, cols], tiles.at[m, buf], tile_sem.at[m, buf])

    def put_rows(k, i, value):
        high, low = split(value)
        to = pl.ds(pl.multiple_of(i * quarter, quarter), quarter)
        right[k, to, :] = high
        right[k + 1, to, :] = low

    def factor_rows(i, carry):
        here = pl.ds(pl.multiple_of(i * quarter, quarter), quarter)
        copy = load(fa_ref.at[here], sa, 0)
        copy.start()
        copy.wait()
        put_rows(0, i, sa[...])
        return carry

    def opened_rows(i, carry):
        here = pl.ds(pl.multiple_of(i * quarter, quarter), quarter)
        copies = [load(uo.at[here], sx, 0), load(ru.at[here], sx2, 1)]
        for copy in copies:
            copy.start()
        for copy in copies:
            copy.wait()
        put_rows(2, i, sx[...] + sx2[...])
        return carry

    def first_tile(t):
        buf = lax.rem(t, 2)
        cols = pl.ds(pl.multiple_of(t * TILE, TILE), TILE)

        @pl.when(t + 1 < nt)
        def _():
            fetch(1, t + 1, lax.rem(t + 1, 2)).start()

        fetch(1, t, buf).wait()
        weight = split(tiles[1, buf].reshape(d, TILE))
        ybuf[:, cols] = ybuf[:, cols] + product((right[0], right[1]), weight)

    def second_tile(t):
        buf = lax.rem(t, 2)
        cols = pl.ds(pl.multiple_of(t * TILE, TILE), TILE)

        @pl.when(t + 1 < nt)
        def _():
            for m in range(2):
                fetch(m, t + 1, lax.rem(t + 1, 2)).start()

        for m in range(2):
            fetch(m, t, buf).wait()
        weight = split(tiles[0, buf].reshape(d, TILE) + keep * tiles[1, buf].reshape(d, TILE))
        ybuf[:, cols] = ybuf[:, cols] + product((right[2], right[3]), weight)
        pltpu.make_async_copy(ybuf.at[:, cols], y_ref.at[:, cols], y_sem.at[t]).start()

    for m in range(2):
        sum_start(m)

    def forward(work):
        @pl.when(work == 0)
        def _():
            fetch(1, 0, 0).start()
            lax.fori_loop(0, 4, factor_rows, 0)
            fetch_y.wait()

        @pl.when(work < nt // 2)
        def _():
            first_tile(2 * work)
            first_tile(2 * work + 1)

        @pl.when(work == late)
        def _():
            for m in range(2):
                fetch(m, 0, 0).start()
            open_copy().wait_recv()
            lax.fori_loop(0, 4, opened_rows, 0)

        @pl.when(jnp.logical_and(work >= late, work < late + nt // 2))
        def _():
            second_tile(2 * (work - late))
            second_tile(2 * (work - late) + 1)

    late = 2 * (steps - 1) - nt // 2 - 1

    def ring_step(step, carry):
        forward(2 * (step - 1))
        sum_step(0, step)
        forward(2 * (step - 1) + 1)
        sum_step(1, step)
        return carry

    lax.fori_loop(1, steps, ring_step, 0)

    def swap_copy(way, sub):
        cols = cols_of(way, sub)
        return remote(give.at[:, cols], got.at[:, cols], sw_send.at[way, sub], sw_recv.at[way, sub], other)

    def total(m, way, sub):
        cols = cols_of(way, sub)
        held = slots.at[m, way, sub, steps - 1]
        sum_copy(m, way, sub, steps - 1, held).wait_recv()
        return slots[m, way, sub, steps - 1] + (acc[m, chip, core, :, cols] + mate[m, chip, :, cols])

    for m in range(2):
        mate_copy(m, chip).wait_recv()
    for sub in range(SUBS):
        for way in range(2):
            cols = cols_of(way, sub)
            give[:, cols] = total(0, way, sub) - keep * bc_ref[:, cols]
            swap_copy(way, sub).start()
    for sub in range(SUBS):
        for way in range(2):
            cols = cols_of(way, sub)
            dw_ref[:, cols] = total(1, way, sub) + keep * bc_ref[:, cols]
    for sub in range(SUBS):
        for way in range(2):
            cols = cols_of(way, sub)
            swap_copy(way, sub).wait_recv()
            dw_ref[:, cols] = dw_ref[:, cols] + got[:, cols]

    def drain(step, carry):
        for m in range(2):
            for way in range(2):
                for sub in range(SUBS):
                    gather_copy(m, way, sub, step).wait_send()
                    sum_copy(m, way, sub, step, slots.at[m, way, sub, step]).wait_send()
        return carry

    lax.fori_loop(0, steps, drain, 0)
    for m in range(2):
        remote(acc.at[m, :, 1 - core], mate.at[m], mt_send.at[m], mt_recv.at[m, 0], buddy).wait_send()
    mask_copy().wait_send()
    open_copy().wait_send()
    for side in range(2):

        @pl.when(party == side)
        def _():
            for j in range(2):
                for copy in chunk_copies(side, j):
                    copy.wait_send()

    for way in range(2):
        for sub in range(SUBS):
            swap_copy(way, sub).wait_send()
    for t in range(nt):
        cols = pl.ds(t * TILE, TILE)
        pltpu.make_async_copy(ybuf.at[:, cols], y_ref.at[:, cols], y_sem.at[t]).wait()


def body(n, x_share, w_share, g_share, fwd_a, fwd_b, fwd_c, bwd_a, bwd_b, bwd_c):
    tokens, d = x_share.shape[1:]
    rows, ff = fwd_b.shape[1:]
    nc = n // 2
    steps = nc - 1
    quarter, eighth = tokens // 4, tokens // 8
    piece = ff // (2 * SUBS)
    hbm = pl.BlockSpec(memory_space=pl.ANY)
    vmem = pl.BlockSpec(memory_space=pltpu.VMEM)
    dma = pltpu.SemaphoreType.DMA

    def shape(*dims):
        return jax.ShapeDtypeStruct(dims, F32)

    outs = pl.pallas_call(
        functools.partial(kernel, n),
        out_shape=[
            shape(tokens, ff),
            shape(rows, ff),
            shape(2, nc, 2, rows, ff),
            shape(tokens, d),
            shape(tokens, d),
            shape(tokens // 4, ff),
            shape(tokens, d),
            shape(tokens, d),
        ],
        in_specs=[hbm] * 6 + [vmem] * 3,
        out_specs=[hbm, vmem] + [hbm] * 6,
        scratch_shapes=[
            pltpu.VMEM((2, nc, 2, rows, ff), F32),
            pltpu.VMEM((2, nc, rows, ff), F32),
            pltpu.VMEM((2, 2, SUBS, steps, rows, piece), F32),
            pltpu.VMEM((3, 2, d, 2 * quarter), BF16),
            pltpu.VMEM((4, 4 * quarter, ff // 2), BF16),
            pltpu.VMEM((quarter, d), F32),
            pltpu.VMEM((quarter, d), F32),
            pltpu.VMEM((quarter, d), F32),
            pltpu.VMEM((quarter, d), F32),
            pltpu.VMEM((quarter, ff), F32),
            pltpu.VMEM((quarter, ff), F32),
            pltpu.VMEM((eighth, ff), F32),
            pltpu.VMEM((2, 2, nc, 2, rows, TILE), F32),
            pltpu.VMEM((tokens, ff), F32),
            pltpu.VMEM((rows, ff), F32),
            pltpu.VMEM((rows, ff), F32),
            pltpu.VMEM((rows, ff), F32),
            pltpu.VMEM((rows, ff), F32),
            pltpu.VMEM((rows, ff), F32),
            dma((7,)),
            dma((2, 2)),
            dma((ff // TILE,)),
            dma((2,)),
            dma((6,)),
            dma((6,)),
            dma((2, SUBS)),
            dma((2, SUBS)),
            dma((2, 2, SUBS, steps)),
            dma((2, 2, SUBS, steps)),
            dma((2,)),
            dma((2,)),
            dma((2, 2, SUBS, steps)),
            dma((2, 2, SUBS, steps)),
            dma((2,)),
            dma((2, nc)),
        ],
        compiler_params=pltpu.CompilerParams(collective_id=0, has_side_effects=True, vmem_limit_bytes=66_500_000),
        cost_estimate=pl.CostEstimate(flops=32 * tokens * d * ff, bytes_accessed=100 * 2**20, transcendentals=0),
    )(
        x_share[0],
        g_share[0],
        fwd_a[0],
        fwd_c[0],
        bwd_a[0],
        bwd_b[0],
        w_share[0],
        fwd_b[0],
        bwd_c[0],
    )
    return outs[0][None], outs[1][None]


def solution(mesh):
    spec = P("party", "dp", None)
    return jax.shard_map(
        functools.partial(body, mesh.shape["dp"]),
        mesh=mesh,
        in_specs=(spec,) * 9,
        out_specs=(spec, spec),
        check_vma=False,
    )
```

```python
import functools

import jax
import jax.numpy as jnp
from jax import lax
from jax.experimental import pallas as pl
from jax.experimental.pallas import tpu as pltpu
from jax.sharding import PartitionSpec as P

MESH = pl.DeviceIdType.MESH
BF16, F32 = jnp.bfloat16, jnp.float32
SUBS = 2
LAG = 2
TILE = 256
WIDE = 1024


def position(chip, nc):
    z, y = chip // 2, lax.rem(chip, 2)
    return z + y * (nc - 1 - 2 * z)


def chip_at(spot, nc):
    spot = lax.rem(spot + 2 * nc, nc)
    y = spot // (nc // 2)
    z = spot + y * (nc - 1 - 2 * spot)
    return 2 * z + y


def split(value):
    high = value.astype(BF16)
    return high, (value - high.astype(F32)).astype(BF16)


def product(left, right):
    def dot(a, b):
        return jnp.dot(a, b, preferred_element_type=F32)

    return dot(left[0], right[0]) + (dot(left[1], right[0]) + dot(left[0], right[1]))


def kernel(
    n,
    x_ref,
    g_ref,
    fa_ref,
    fc_ref,
    ba_ref,
    bb_ref,
    w_ref,
    fb_ref,
    bc_ref,
    y_ref,
    dw_ref,
    wts,
    rx,
    ra,
    rg,
    uo,
    ru,
    acc,
    mate,
    slots,
    lefts,
    right,
    sx,
    sx2,
    sa,
    sa2,
    sg,
    sb,
    sg2,
    tiles,
    ybuf,
    own_w,
    got_w,
    delta,
    give,
    got,
    ld_sem,
    tile_sem,
    y_sem,
    lc_sem,
    xs_send,
    xs_recv,
    sw_send,
    sw_recv,
    ag_send,
    ag_recv,
    ac_send,
    ac_recv,
    rs_send,
    rs_recv,
    mt_send,
    mt_recv,
):
    nc = n // 2
    steps = nc - 1
    party, me = lax.axis_index("party"), lax.axis_index("dp")
    core, chip = lax.rem(me, 2), me // 2
    spot = position(chip, nc)
    rows, ff = fb_ref.shape
    tokens, d = x_ref.shape
    quarter, eighth = tokens // 4, tokens // 8
    piece = ff // (2 * SUBS)
    first = party == 0
    other = {"party": 1 - party}
    buddy = {"dp": me + 1 - 2 * core}
    ahead = {"dp": 2 * chip_at(spot + 1, nc) + core}
    behind = {"dp": 2 * chip_at(spot - 1, nc) + core}

    def cols_of(way, sub):
        return pl.ds((way * SUBS + sub) * piece, piece)

    def half_of(way):
        return pl.ds(way * (ff // 2), ff // 2)

    def remote(src, dst, send, recv, device):
        return pltpu.make_async_remote_copy(
            src_ref=src, dst_ref=dst, send_sem=send, recv_sem=recv, device_id=device, device_id_type=MESH
        )

    own_w[...] = w_ref[...] - fb_ref[...]
    barrier = pltpu.get_barrier_semaphore()
    for device in (other, buddy, ahead, behind):
        pl.semaphore_signal(barrier, inc=1, device_id=device, device_id_type=MESH)
    pl.semaphore_wait(barrier, 4)

    def chunk_copies(side, j):
        start = j * 2 * quarter
        k = 1 + 2 * j
        if side == 0:
            everything = pl.ds(start, 2 * quarter)
            tail = pl.ds(start + 3 * eighth, eighth)
            return [
                remote(x_ref.at[everything], rx.at[everything], xs_send.at[k], xs_recv.at[k], other),
                remote(g_ref.at[tail], rg.at[pl.ds(j * eighth, eighth)], xs_send.at[k + 1], xs_recv.at[k + 1], other),
            ]
        head = pl.ds(start, 3 * eighth)
        return [
            remote(x_ref.at[head], rx.at[head], xs_send.at[k], xs_recv.at[k], other),
            remote(ba_ref.at[head], ra.at[head], xs_send.at[k + 1], xs_recv.at[k + 1], other),
        ]

    def mask_copy():
        return remote(own_w, got_w, xs_send.at[0], xs_recv.at[0], other)

    def open_copy():
        return remote(uo, ru, xs_send.at[5], xs_recv.at[5], other)

    def gather_copy(m, way, sub, step):
        owner = chip_at(spot - step, nc) if way == 0 else chip_at(spot + step, nc)
        return remote(
            wts.at[m, owner, core, :, cols_of(way, sub)],
            wts.at[m, owner, core, :, cols_of(way, sub)],
            ag_send.at[m, way, sub, step],
            ag_recv.at[m, way, sub, step],
            ahead if way == 0 else behind,
        )

    def gather_first(m, way, sub, source):
        return remote(
            source.at[:, cols_of(way, sub)],
            wts.at[m, chip, core, :, cols_of(way, sub)],
            ag_send.at[m, way, sub, 0],
            ag_recv.at[m, way, sub, 0],
            ahead if way == 0 else behind,
        )

    def gather_arrival(m, way, sub, step):
        owner = chip_at(spot - 1 - step, nc) if way == 0 else chip_at(spot + 1 + step, nc)
        here = wts.at[m, owner, core, :, cols_of(way, sub)]
        return remote(here, here, ag_send.at[m, way, sub, step], ag_recv.at[m, way, sub, step], ahead)

    def begin_gather(m, source):
        for sub in range(SUBS):
            for way in range(2):
                gather_first(m, way, sub, source).start()
        remote(source, wts.at[m, chip, core], ac_send.at[m], ac_recv.at[m], buddy).start()
        pltpu.make_async_copy(source, wts.at[m, chip, core], lc_sem.at[m]).start()

    def pass_on(m, step):
        for sub in range(SUBS):
            for way in range(2):
                gather_arrival(m, way, sub, step).wait_recv()

                @pl.when(step < steps - 1)
                def _():
                    gather_copy(m, way, sub, step + 1).start()

        for way in range(2):
            owner = chip_at(spot - 1 - step, nc) if way == 0 else chip_at(spot + 1 + step, nc)
            here = wts.at[m, owner, core, :, half_of(way)]
            remote(here, here, ac_send.at[m], ac_recv.at[m], buddy).start()

    def load(src, dst, k):
        return pltpu.make_async_copy(src, dst, ld_sem.at[k])

    def open_rows(i):
        part = pl.ds(pl.multiple_of(i * quarter, 8), quarter)
        at = pl.ds(0, quarter)
        copies = [load(x_ref.at[part], sx.at[at], 0), load(fa_ref.at[part], sa.at[at], 1)]
        for copy in copies:
            copy.start()
        for copy in copies:
            copy.wait()
        sx2[:quarter, :] = sx[:quarter, :] - sa[:quarter, :]
        out = load(sx2.at[at], uo.at[part], 2)
        out.start()
        out.wait()

    def put_left(k, at, value):
        high, low = split(value)
        lefts[k, 0, :, at] = high.T
        lefts[k, 1, :, at] = low.T

    def put_right(k, at, value):
        high, low = split(value)
        for half in range(2):
            to = slice(half * 2 * quarter + at.start, half * 2 * quarter + at.stop)
            right[2 * k, to, :] = high[:, half * (ff // 2) : (half + 1) * (ff // 2)]
            right[2 * k + 1, to, :] = low[:, half * (ff // 2) : (half + 1) * (ff // 2)]

    def owned(j):
        start = 2 * j * quarter
        both = pl.ds(start, 2 * quarter)
        rest = [load(x_ref.at[both], sx, 0), load(ba_ref.at[both], sa, 1)]
        for copy in rest:
            copy.start()
        for part in range(2):
            here = pl.ds(start + part * quarter, quarter)
            to = slice(part * quarter, (part + 1) * quarter)
            own = [load(g_ref.at[here], sg, 2), load(bb_ref.at[here], sb, 3)]
            for copy in own:
                copy.start()
            for copy in own:
                copy.wait()
            put_right(1, to, sb[...])

            @pl.when(first)
            def _():
                if part == 1:
                    sg[eighth:, :] = jnp.zeros((eighth, ff), F32)
                put_right(0, to, sg[...])

            @pl.when(jnp.logical_not(first))
            def _():
                sg[...] = sg[...] - sb[...]
                put_right(0, to, sg[...])

        for copy in rest:
            copy.wait()
        whole = slice(0, 2 * quarter)

        @pl.when(first)
        def _():
            put_left(2, whole, sa[...])

        @pl.when(jnp.logical_not(first))
        def _():
            put_left(1, whole, sa[...])

    def received(j):
        start = 2 * j * quarter
        whole = slice(0, 2 * quarter)
        many = 3 * eighth

        @pl.when(first)
        def _():
            for copy in chunk_copies(1, j):
                copy.wait_recv()
            some = pl.ds(start, many)
            more = [load(rx.at[some], sx2.at[pl.ds(0, many)], 4), load(ra.at[some], sa2.at[pl.ds(0, many)], 5)]
            for copy in more:
                copy.start()
            for copy in more:
                copy.wait()
            sx2[many:, :] = jnp.zeros((eighth, d), F32)
            sa2[many:, :] = jnp.zeros((eighth, d), F32)
            sx[many:, :] = jnp.zeros((eighth, d), F32)
            put_left(0, whole, sa2[...])
            put_left(1, whole, (sx[...] + sx2[...]) - sa2[...])

        @pl.when(jnp.logical_not(first))
        def _():
            for copy in chunk_copies(0, j):
                copy.wait_recv()
            more = [
                load(rx.at[pl.ds(start, 2 * quarter)], sx2, 4),
                load(rg.at[pl.ds(j * eighth, eighth)], sg2, 5),
            ]
            for copy in more:
                copy.start()
            for copy in more:
                copy.wait()
            put_right(0, slice(many, 2 * quarter), sg[eighth:, :] + sg2[...])
            sx[...] = sx[...] + sx2[...]
            put_left(0, whole, sx[...] - sa[...])
            put_left(2, whole, sx[...])

    keep = jnp.where(first, 1.0, 0.0).astype(F32)
    sign = 1.0 - 2.0 * keep
    group = d // 4
    per = group // (2 * rows)

    def gradient_rows(j, q, tile_from, tile_to):
        at = pl.ds(pl.multiple_of(q * group, group), group)
        chips = pl.ds(q * per, per)

        def tile(t, carry):
            half = t // (ff // 2 // WIDE)
            deep = pl.ds(pl.multiple_of(half * 2 * quarter, 2 * quarter), 2 * quarter)
            wide = pl.ds(pl.multiple_of(lax.rem(t, ff // 2 // WIDE) * WIDE, WIDE), WIDE)
            cols = pl.ds(pl.multiple_of(t * WIDE, WIDE), WIDE)

            def multiply(k, m):
                return product(
                    (lefts[k, 0, at, :], lefts[k, 1, at, :]),
                    (right[2 * m, deep, wide], right[2 * m + 1, deep, wide]),
                )

            shared = multiply(2, 1)
            shape = (per, 2, rows, WIDE)
            foreign = (multiply(0, 0) + keep * shared).reshape(shape)
            mine = (multiply(1, 0) + sign * shared).reshape(shape)
            if j == 0:
                acc[0, chips, :, :, cols] = foreign
                acc[1, chips, :, :, cols] = mine
            else:
                acc[0, chips, :, :, cols] = acc[0, chips, :, :, cols] + foreign
                acc[1, chips, :, :, cols] = acc[1, chips, :, :, cols] + mine
            return carry

        lax.fori_loop(tile_from, tile_to, tile, 0)

    begin_gather(0, fb_ref)
    mask_copy().start()
    for side in range(2):

        @pl.when(party == side)
        def _():
            for j in range(2):
                for copy in chunk_copies(side, j):
                    copy.start()

    early = steps - 3

    def gather_step(i, carry):
        @pl.when(i < steps)
        def _():
            pass_on(0, i)

        @pl.when(i < 4)
        def _():
            open_rows(i)

        @pl.when(i == 3)
        def _():
            open_copy().start()

        @pl.when(i == early)
        def _():
            owned(0)
            received(0)

        @pl.when(i > early)
        def _():
            @pl.when(i <= early + 2)
            def _():
                gradient_rows(0, 2 * (i - early - 1), 0, ff // WIDE)

        @pl.when(i == LAG - 1)
        def _():
            mask_copy().wait_recv()
            delta[...] = own_w[...] + got_w[...]
            begin_gather(1, delta)

        @pl.when(i >= LAG)
        def _():
            pass_on(1, i - LAG)

        @pl.when(i > early)
        def _():
            @pl.when(i <= early + 2)
            def _():
                gradient_rows(0, 2 * (i - early - 1) + 1, 0, ff // WIDE)

        return carry

    lax.fori_loop(0, steps + LAG - 1, gather_step, 0)

    owned(1)
    received(1)
    zs, span = nc // 2, nc // 8

    def group_at(way, k):
        place = jnp.where(way == 0, spot, nc - 1 - spot)
        falling = (place + span - 1) // span
        rising = (nc - place) // span
        low = jnp.where(k < falling, falling - 1 - k, k)
        high = jnp.where(k < 4 - rising, rising + k, 3 - k)
        return jnp.where(place <= zs, low, high)

    def mate_copy(m, way, k):
        chips = pl.ds(group_at(way, k) * per, per)
        cols = pl.ds(pl.multiple_of(way * (ff // 2), 128), ff // 2)
        return remote(
            acc.at[m, chips, 1 - core, :, cols],
            mate.at[m, chips, :, cols],
            mt_send.at[m, way, k],
            mt_recv.at[m, way, k],
            buddy,
        )

    def second(k):
        def one(way, carry):
            gradient_rows(1, group_at(way, k), way * (ff // 2 // WIDE), (way + 1) * (ff // 2 // WIDE))
            for m in range(2):
                mate_copy(m, way, k).start()
            return carry

        lax.fori_loop(0, 2, one, 0)

    fetch_y = load(fc_ref, ybuf, 6)
    fetch_y.start()

    def owner_of(way, step):
        return chip_at(spot - 1 - step, nc) if way == 0 else chip_at(spot + 1 + step, nc)

    def sum_copy(m, way, sub, step, source):
        return remote(
            source,
            slots.at[m, way, sub, step],
            rs_send.at[m, way, sub, step],
            rs_recv.at[m, way, sub, step],
            ahead if way == 0 else behind,
        )

    def mate_arrivals(m, step):
        for way in range(2):
            mate_copy(m, way, step).wait_recv()

    def sum_start(m):
        mate_arrivals(m, 0)
        for sub in range(SUBS):
            for way in range(2):
                owner, cols = owner_of(way, 0), cols_of(way, sub)
                acc[m, owner, core, :, cols] = acc[m, owner, core, :, cols] + mate[m, owner, :, cols]
                sum_copy(m, way, sub, 0, acc.at[m, owner, core, :, cols]).start()

    def sum_step(m, step):
        @pl.when(step < 4)
        def _():
            mate_arrivals(m, step)

        for sub in range(SUBS):
            for way in range(2):
                owner, cols = owner_of(way, step), cols_of(way, sub)
                held = slots.at[m, way, sub, step - 1]
                sum_copy(m, way, sub, step - 1, held).wait_recv()
                slots[m, way, sub, step - 1] = slots[m, way, sub, step - 1] + (
                    acc[m, owner, core, :, cols] + mate[m, owner, :, cols]
                )
                sum_copy(m, way, sub, step, held).start()

    nt = ff // TILE

    def fetch(m, t, buf):
        cols = pl.ds(pl.multiple_of(t * TILE, TILE), TILE)
        return pltpu.make_async_copy(wts.at[m, :, :, :, cols], tiles.at[m, buf], tile_sem.at[m, buf])

    def put_rows(k, i, value):
        high, low = split(value)
        to = pl.ds(i * 2 * quarter, 2 * quarter)
        right[k, to, :] = high
        right[k + 1, to, :] = low

    def factor_rows(i):
        here = pl.ds(i * 2 * quarter, 2 * quarter)
        copy = load(fa_ref.at[here], sa, 0)
        copy.start()
        copy.wait()
        put_rows(0, i, sa[...])

    def opened_rows(i):
        here = pl.ds(i * 2 * quarter, 2 * quarter)
        copies = [load(uo.at[here], sx, 0), load(ru.at[here], sx2, 1)]
        for copy in copies:
            copy.start()
        for copy in copies:
            copy.wait()
        put_rows(2, i, sx[...] + sx2[...])

    def first_tile(t):
        buf = lax.rem(t, 2)
        cols = pl.ds(pl.multiple_of(t * TILE, TILE), TILE)

        @pl.when(t + 1 < nt)
        def _():
            fetch(1, t + 1, 1 - buf).start()

        fetch(1, t, buf).wait()
        weight = split(tiles[1, buf].reshape(d, TILE))
        ybuf[:, cols] = ybuf[:, cols] + product((right[0], right[1]), weight)

    def second_tile(t):
        buf = lax.rem(t, 2)
        cols = pl.ds(pl.multiple_of(t * TILE, TILE), TILE)

        @pl.when(t + 1 < nt)
        def _():
            for m in range(2):
                fetch(m, t + 1, 1 - buf).start()

        for m in range(2):
            fetch(m, t, buf).wait()
        weight = split(tiles[0, buf].reshape(d, TILE) + keep * tiles[1, buf].reshape(d, TILE))
        ybuf[:, cols] = ybuf[:, cols] + product((right[2], right[3]), weight)
        pltpu.make_async_copy(ybuf.at[:, cols], y_ref.at[:, cols], y_sem.at[t]).start()

    second(0)
    sum_start(0)
    second(1)
    pass_on(1, steps - 1)
    late = 2 * steps - 6

    def several(tile, turn):
        def one(t, carry):
            tile(t)
            return carry

        lax.fori_loop(turn * nt // 3, (turn + 1) * nt // 3, one, 0)

    def forward(work):
        @pl.when(work == 3)
        def _():
            for m in range(2):
                pltpu.make_async_copy(wts.at[m, chip, core], wts.at[m, chip, core], lc_sem.at[m]).wait()
                everything = remote(wts.at[m, :, core], wts.at[m, :, 1 - core], ac_send.at[m], ac_recv.at[m], buddy)
                everything.wait_recv()
                everything.wait_send()
            fetch(1, 0, 0).start()
            fetch_y.wait()

        @pl.when(work == 4)
        def _():
            factor_rows(0)
            factor_rows(1)

        @pl.when(jnp.logical_and(work >= 5, work < 8))
        def _():
            several(first_tile, work - 5)

        @pl.when(jnp.logical_and(work > late, work <= late + 3))
        def _():
            several(second_tile, work - late - 1)

        @pl.when(work == late)
        def _():
            for m in range(2):
                fetch(m, 0, 0).start()
            open_copy().wait_recv()
            for i in range(2):
                opened_rows(i)

    def swap_copy(way, sub):
        cols = cols_of(way, sub)
        return remote(give.at[:, cols], got.at[:, cols], sw_send.at[way, sub], sw_recv.at[way, sub], other)

    def total(m, way, sub):
        cols = cols_of(way, sub)
        held = slots.at[m, way, sub, steps - 1]
        sum_copy(m, way, sub, steps - 1, held).wait_recv()
        return slots[m, way, sub, steps - 1] + (acc[m, chip, core, :, cols] + mate[m, chip, :, cols])

    def half_step(work, carry):
        m = lax.rem(work, 2)
        step = work // 2 + 1 - m
        forward(work)

        @pl.when(jnp.logical_and(m == 1, step < 2))
        def _():
            second(step + 2)

        @pl.when(step == 0)
        def _():
            sum_start(1)

        @pl.when(jnp.logical_and(step > 0, step < steps))
        def _():
            sum_step(m, step)

        @pl.when(step == steps)
        def _():
            for sub in range(SUBS):
                for way in range(2):
                    cols = cols_of(way, sub)
                    give[:, cols] = total(0, way, sub) - keep * bc_ref[:, cols]
                    swap_copy(way, sub).start()

        return carry

    lax.fori_loop(0, 2 * steps, half_step, 0)
    for sub in range(SUBS):
        for way in range(2):
            cols = cols_of(way, sub)
            dw_ref[:, cols] = total(1, way, sub) + keep * bc_ref[:, cols]
    for sub in range(SUBS):
        for way in range(2):
            cols = cols_of(way, sub)
            swap_copy(way, sub).wait_recv()
            dw_ref[:, cols] = dw_ref[:, cols] + got[:, cols]

    def drain(step, carry):
        for m in range(2):
            for way in range(2):
                for sub in range(SUBS):
                    gather_copy(m, way, sub, step).wait_send()
                    sum_copy(m, way, sub, step, slots.at[m, way, sub, step]).wait_send()
        return carry

    lax.fori_loop(0, steps, drain, 0)
    for m in range(2):
        for way in range(2):
            for k in range(4):
                mate_copy(m, way, k).wait_send()
    mask_copy().wait_send()
    open_copy().wait_send()
    for side in range(2):

        @pl.when(party == side)
        def _():
            for j in range(2):
                for copy in chunk_copies(side, j):
                    copy.wait_send()

    for way in range(2):
        for sub in range(SUBS):
            swap_copy(way, sub).wait_send()
    for t in range(nt):
        cols = pl.ds(t * TILE, TILE)
        pltpu.make_async_copy(ybuf.at[:, cols], y_ref.at[:, cols], y_sem.at[t]).wait()


def body(n, x_share, w_share, g_share, fwd_a, fwd_b, fwd_c, bwd_a, bwd_b, bwd_c):
    tokens, d = x_share.shape[1:]
    rows, ff = fwd_b.shape[1:]
    nc = n // 2
    steps = nc - 1
    quarter, eighth = tokens // 4, tokens // 8
    piece = ff // (2 * SUBS)
    hbm = pl.BlockSpec(memory_space=pl.ANY)
    vmem = pl.BlockSpec(memory_space=pltpu.VMEM)
    dma = pltpu.SemaphoreType.DMA

    def shape(*dims):
        return jax.ShapeDtypeStruct(dims, F32)

    outs = pl.pallas_call(
        functools.partial(kernel, n),
        out_shape=[
            shape(tokens, ff),
            shape(rows, ff),
            shape(2, nc, 2, rows, ff),
            shape(tokens, d),
            shape(tokens, d),
            shape(tokens // 4, ff),
            shape(tokens, d),
            shape(tokens, d),
        ],
        in_specs=[hbm] * 6 + [vmem] * 3,
        out_specs=[hbm, vmem] + [hbm] * 6,
        scratch_shapes=[
            pltpu.VMEM((2, nc, 2, rows, ff), F32),
            pltpu.VMEM((2, nc, rows, ff), F32),
            pltpu.VMEM((2, 2, SUBS, steps, rows, piece), F32),
            pltpu.VMEM((3, 2, d, 2 * quarter), BF16),
            pltpu.VMEM((4, 4 * quarter, ff // 2), BF16),
            pltpu.VMEM((2 * quarter, d), F32),
            pltpu.VMEM((2 * quarter, d), F32),
            pltpu.VMEM((2 * quarter, d), F32),
            pltpu.VMEM((2 * quarter, d), F32),
            pltpu.VMEM((quarter, ff), F32),
            pltpu.VMEM((quarter, ff), F32),
            pltpu.VMEM((eighth, ff), F32),
            pltpu.VMEM((2, 2, nc, 2, rows, TILE), F32),
            pltpu.VMEM((tokens, ff), F32),
            pltpu.VMEM((rows, ff), F32),
            pltpu.VMEM((rows, ff), F32),
            pltpu.VMEM((rows, ff), F32),
            pltpu.VMEM((rows, ff), F32),
            pltpu.VMEM((rows, ff), F32),
            dma((7,)),
            dma((2, 2)),
            dma((ff // TILE,)),
            dma((2,)),
            dma((6,)),
            dma((6,)),
            dma((2, SUBS)),
            dma((2, SUBS)),
            dma((2, 2, SUBS, steps)),
            dma((2, 2, SUBS, steps)),
            dma((2,)),
            dma((2,)),
            dma((2, 2, SUBS, steps)),
            dma((2, 2, SUBS, steps)),
            dma((2, 2, 4)),
            dma((2, 2, 4)),
        ],
        compiler_params=pltpu.CompilerParams(collective_id=0, has_side_effects=True, vmem_limit_bytes=66_500_000),
        cost_estimate=pl.CostEstimate(flops=32 * tokens * d * ff, bytes_accessed=100 * 2**20, transcendentals=0),
    )(
        x_share[0],
        g_share[0],
        fwd_a[0],
        fwd_c[0],
        bwd_a[0],
        bwd_b[0],
        w_share[0],
        fwd_b[0],
        bwd_c[0],
    )
    return outs[0][None], outs[1][None]


def solution(mesh):
    spec = P("party", "dp", None)
    return jax.shard_map(
        functools.partial(body, mesh.shape["dp"]),
        mesh=mesh,
        in_specs=(spec,) * 9,
        out_specs=(spec, spec),
        check_vma=False,
    )
```

```python
import functools

import jax
import jax.numpy as jnp
from jax import lax
from jax.experimental import pallas as pl
from jax.experimental.pallas import tpu as pltpu
from jax.sharding import PartitionSpec as P

MESH = pl.DeviceIdType.MESH
BF16, F32 = jnp.bfloat16, jnp.float32
SUBS = 2
LAG = 2
TILE = 256
WIDE = 1024


def position(chip, nc):
    z, y = chip // 2, lax.rem(chip, 2)
    return z + y * (nc - 1 - 2 * z)


def chip_at(spot, nc):
    spot = lax.rem(spot + 2 * nc, nc)
    y = spot // (nc // 2)
    z = spot + y * (nc - 1 - 2 * spot)
    return 2 * z + y


def split(value):
    high = value.astype(BF16)
    return high, (value - high.astype(F32)).astype(BF16)


def product(left, right):
    def dot(a, b):
        return jnp.dot(a, b, preferred_element_type=F32)

    return dot(left[0], right[0]) + (dot(left[1], right[0]) + dot(left[0], right[1]))


def kernel(
    n,
    x_ref,
    g_ref,
    fa_ref,
    fc_ref,
    ba_ref,
    bb_ref,
    w_ref,
    fb_ref,
    bc_ref,
    ybuf,
    dw_ref,
    wts,
    rx,
    ra,
    rg,
    uo,
    ru,
    acc,
    mate,
    slots,
    lefts,
    right,
    sx,
    sx2,
    sa,
    sa2,
    sg,
    sb,
    sg2,
    tiles,
    own_w,
    got_w,
    delta,
    give,
    got,
    ld_sem,
    tile_sem,
    lc_sem,
    xs_send,
    xs_recv,
    sw_send,
    sw_recv,
    ag_send,
    ag_recv,
    ac_send,
    ac_recv,
    rs_send,
    rs_recv,
    mt_send,
    mt_recv,
):
    nc = n // 2
    steps = nc - 1
    party, me = lax.axis_index("party"), lax.axis_index("dp")
    core, chip = lax.rem(me, 2), me // 2
    spot = position(chip, nc)
    rows, ff = fb_ref.shape
    tokens, d = x_ref.shape
    quarter, eighth = tokens // 4, tokens // 8
    piece = ff // (2 * SUBS)
    first = party == 0
    other = {"party": 1 - party}
    buddy = {"dp": me + 1 - 2 * core}
    ahead = {"dp": 2 * chip_at(spot + 1, nc) + core}
    behind = {"dp": 2 * chip_at(spot - 1, nc) + core}

    def cols_of(way, sub):
        return pl.ds((way * SUBS + sub) * piece, piece)

    def half_of(way):
        return pl.ds(way * (ff // 2), ff // 2)

    def remote(src, dst, send, recv, device):
        return pltpu.make_async_remote_copy(
            src_ref=src, dst_ref=dst, send_sem=send, recv_sem=recv, device_id=device, device_id_type=MESH
        )

    masks = [pltpu.make_async_copy(w_ref, own_w, ld_sem.at[0]), pltpu.make_async_copy(fb_ref, delta, ld_sem.at[1])]
    for copy in masks:
        copy.start()
    barrier = pltpu.get_barrier_semaphore()
    for device in (other, buddy, ahead, behind):
        pl.semaphore_signal(barrier, inc=1, device_id=device, device_id_type=MESH)
    pl.semaphore_wait(barrier, 4)

    def chunk_copies(side, j):
        start = j * 2 * quarter
        k = 1 + 2 * j
        if side == 0:
            everything = pl.ds(start, 2 * quarter)
            tail = pl.ds(start + 3 * eighth, eighth)
            return [
                remote(x_ref.at[everything], rx.at[everything], xs_send.at[k], xs_recv.at[k], other),
                remote(g_ref.at[tail], rg.at[pl.ds(j * eighth, eighth)], xs_send.at[k + 1], xs_recv.at[k + 1], other),
            ]
        head = pl.ds(start, 3 * eighth)
        return [
            remote(x_ref.at[head], rx.at[head], xs_send.at[k], xs_recv.at[k], other),
            remote(ba_ref.at[head], ra.at[head], xs_send.at[k + 1], xs_recv.at[k + 1], other),
        ]

    def mask_copy():
        return remote(own_w, got_w, xs_send.at[0], xs_recv.at[0], other)

    def open_copy():
        return remote(uo, ru, xs_send.at[5], xs_recv.at[5], other)

    def gather_copy(m, way, sub, step):
        owner = chip_at(spot - step, nc) if way == 0 else chip_at(spot + step, nc)
        return remote(
            wts.at[m, owner, core, :, cols_of(way, sub)],
            wts.at[m, owner, core, :, cols_of(way, sub)],
            ag_send.at[m, way, sub, step],
            ag_recv.at[m, way, sub, step],
            ahead if way == 0 else behind,
        )

    def gather_first(m, way, sub, source):
        return remote(
            source.at[:, cols_of(way, sub)],
            wts.at[m, chip, core, :, cols_of(way, sub)],
            ag_send.at[m, way, sub, 0],
            ag_recv.at[m, way, sub, 0],
            ahead if way == 0 else behind,
        )

    def gather_arrival(m, way, sub, step):
        owner = chip_at(spot - 1 - step, nc) if way == 0 else chip_at(spot + 1 + step, nc)
        here = wts.at[m, owner, core, :, cols_of(way, sub)]
        return remote(here, here, ag_send.at[m, way, sub, step], ag_recv.at[m, way, sub, step], ahead)

    def begin_gather(m, source):
        for sub in range(SUBS):
            for way in range(2):
                gather_first(m, way, sub, source).start()
        remote(source, wts.at[m, chip, core], ac_send.at[m], ac_recv.at[m], buddy).start()
        pltpu.make_async_copy(source, wts.at[m, chip, core], lc_sem.at[m]).start()

    def pass_on(m, step):
        for sub in range(SUBS):
            for way in range(2):
                gather_arrival(m, way, sub, step).wait_recv()

                @pl.when(step < steps - 1)
                def _():
                    gather_copy(m, way, sub, step + 1).start()

        for way in range(2):
            owner = chip_at(spot - 1 - step, nc) if way == 0 else chip_at(spot + 1 + step, nc)
            here = wts.at[m, owner, core, :, half_of(way)]
            remote(here, here, ac_send.at[m], ac_recv.at[m], buddy).start()

    def load(src, dst, k):
        return pltpu.make_async_copy(src, dst, ld_sem.at[k])

    def open_rows(i):
        part = pl.ds(pl.multiple_of(i * quarter, 8), quarter)
        at = pl.ds(0, quarter)
        copies = [load(x_ref.at[part], sx.at[at], 0), load(fa_ref.at[part], sa.at[at], 1)]
        for copy in copies:
            copy.start()
        for copy in copies:
            copy.wait()
        sx2[:quarter, :] = sx[:quarter, :] - sa[:quarter, :]
        out = load(sx2.at[at], uo.at[part], 2)
        out.start()
        out.wait()

    def put_left(k, at, value):
        high, low = split(value)
        lefts[k, 0, :, at] = high.T
        lefts[k, 1, :, at] = low.T

    def put_right(k, at, value):
        high, low = split(value)
        for half in range(2):
            to = slice(half * 2 * quarter + at.start, half * 2 * quarter + at.stop)
            right[2 * k, to, :] = high[:, half * (ff // 2) : (half + 1) * (ff // 2)]
            right[2 * k + 1, to, :] = low[:, half * (ff // 2) : (half + 1) * (ff // 2)]

    def owned(j):
        start = 2 * j * quarter
        both = pl.ds(start, 2 * quarter)
        rest = [load(x_ref.at[both], sx, 0), load(ba_ref.at[both], sa, 1)]
        for copy in rest:
            copy.start()
        for part in range(2):
            here = pl.ds(start + part * quarter, quarter)
            to = slice(part * quarter, (part + 1) * quarter)
            own = [load(g_ref.at[here], sg, 2), load(bb_ref.at[here], sb, 3)]
            for copy in own:
                copy.start()
            for copy in own:
                copy.wait()
            put_right(1, to, sb[...])

            @pl.when(first)
            def _():
                if part == 1:
                    sg[eighth:, :] = jnp.zeros((eighth, ff), F32)
                put_right(0, to, sg[...])

            @pl.when(jnp.logical_not(first))
            def _():
                sg[...] = sg[...] - sb[...]
                put_right(0, to, sg[...])

        for copy in rest:
            copy.wait()
        whole = slice(0, 2 * quarter)

        @pl.when(first)
        def _():
            put_left(2, whole, sa[...])

        @pl.when(jnp.logical_not(first))
        def _():
            put_left(1, whole, sa[...])

    def received(j):
        start = 2 * j * quarter
        whole = slice(0, 2 * quarter)
        many = 3 * eighth

        @pl.when(first)
        def _():
            for copy in chunk_copies(1, j):
                copy.wait_recv()
            some = pl.ds(start, many)
            more = [load(rx.at[some], sx2.at[pl.ds(0, many)], 4), load(ra.at[some], sa2.at[pl.ds(0, many)], 5)]
            for copy in more:
                copy.start()
            for copy in more:
                copy.wait()
            sx2[many:, :] = jnp.zeros((eighth, d), F32)
            sa2[many:, :] = jnp.zeros((eighth, d), F32)
            sx[many:, :] = jnp.zeros((eighth, d), F32)
            put_left(0, whole, sa2[...])
            put_left(1, whole, (sx[...] + sx2[...]) - sa2[...])

        @pl.when(jnp.logical_not(first))
        def _():
            for copy in chunk_copies(0, j):
                copy.wait_recv()
            more = [
                load(rx.at[pl.ds(start, 2 * quarter)], sx2, 4),
                load(rg.at[pl.ds(j * eighth, eighth)], sg2, 5),
            ]
            for copy in more:
                copy.start()
            for copy in more:
                copy.wait()
            put_right(0, slice(many, 2 * quarter), sg[eighth:, :] + sg2[...])
            sx[...] = sx[...] + sx2[...]
            put_left(0, whole, sx[...] - sa[...])
            put_left(2, whole, sx[...])

    keep = jnp.where(first, 1.0, 0.0).astype(F32)
    sign = 1.0 - 2.0 * keep
    group = d // 4
    per = group // (2 * rows)

    def gradient_rows(j, q, tile_from, tile_to):
        at = pl.ds(pl.multiple_of(q * group, group), group)
        chips = pl.ds(q * per, per)

        def tile(t, carry):
            half = t // (ff // 2 // WIDE)
            deep = pl.ds(pl.multiple_of(half * 2 * quarter, 2 * quarter), 2 * quarter)
            wide = pl.ds(pl.multiple_of(lax.rem(t, ff // 2 // WIDE) * WIDE, WIDE), WIDE)
            cols = pl.ds(pl.multiple_of(t * WIDE, WIDE), WIDE)

            def multiply(k, m):
                return product(
                    (lefts[k, 0, at, :], lefts[k, 1, at, :]),
                    (right[2 * m, deep, wide], right[2 * m + 1, deep, wide]),
                )

            shared = multiply(2, 1)
            shape = (per, 2, rows, WIDE)
            foreign = (multiply(0, 0) + keep * shared).reshape(shape)
            mine = (multiply(1, 0) + sign * shared).reshape(shape)
            if j == 0:
                acc[0, chips, :, :, cols] = foreign
                acc[1, chips, :, :, cols] = mine
            else:
                acc[0, chips, :, :, cols] = acc[0, chips, :, :, cols] + foreign
                acc[1, chips, :, :, cols] = acc[1, chips, :, :, cols] + mine
            return carry

        lax.fori_loop(tile_from, tile_to, tile, 0)

    begin_gather(0, fb_ref)
    for copy in masks:
        copy.wait()
    own_w[...] = own_w[...] - delta[...]
    mask_copy().start()
    for side in range(2):

        @pl.when(party == side)
        def _():
            for j in range(2):
                for copy in chunk_copies(side, j):
                    copy.start()

    early = steps - 3

    def gather_step(i, carry):
        @pl.when(i < steps)
        def _():
            pass_on(0, i)

        @pl.when(i < 4)
        def _():
            open_rows(i)

        @pl.when(i == 3)
        def _():
            open_copy().start()

        @pl.when(i == early)
        def _():
            owned(0)
            received(0)

        @pl.when(i > early)
        def _():
            @pl.when(i <= early + 2)
            def _():
                gradient_rows(0, 2 * (i - early - 1), 0, ff // WIDE)

        @pl.when(i == LAG - 1)
        def _():
            mask_copy().wait_recv()
            delta[...] = own_w[...] + got_w[...]
            begin_gather(1, delta)

        @pl.when(i >= LAG)
        def _():
            pass_on(1, i - LAG)

        @pl.when(i > early)
        def _():
            @pl.when(i <= early + 2)
            def _():
                gradient_rows(0, 2 * (i - early - 1) + 1, 0, ff // WIDE)

        return carry

    lax.fori_loop(0, steps + LAG - 1, gather_step, 0)

    owned(1)
    received(1)
    zs, span = nc // 2, nc // 8

    def group_at(way, k):
        place = jnp.where(way == 0, spot, nc - 1 - spot)
        falling = (place + span - 1) // span
        rising = (nc - place) // span
        low = jnp.where(k < falling, falling - 1 - k, k)
        high = jnp.where(k < 4 - rising, rising + k, 3 - k)
        return jnp.where(place <= zs, low, high)

    def mate_copy(m, way, k):
        chips = pl.ds(group_at(way, k) * per, per)
        cols = pl.ds(pl.multiple_of(way * (ff // 2), 128), ff // 2)
        return remote(
            acc.at[m, chips, 1 - core, :, cols],
            mate.at[m, chips, :, cols],
            mt_send.at[m, way, k],
            mt_recv.at[m, way, k],
            buddy,
        )

    def second(k):
        def one(way, carry):
            gradient_rows(1, group_at(way, k), way * (ff // 2 // WIDE), (way + 1) * (ff // 2 // WIDE))
            for m in range(2):
                mate_copy(m, way, k).start()
            return carry

        lax.fori_loop(0, 2, one, 0)

    fetch_y = load(fc_ref, ybuf, 6)
    fetch_y.start()

    def owner_of(way, step):
        return chip_at(spot - 1 - step, nc) if way == 0 else chip_at(spot + 1 + step, nc)

    def sum_copy(m, way, sub, step, source):
        return remote(
            source,
            slots.at[m, way, sub, step],
            rs_send.at[m, way, sub, step],
            rs_recv.at[m, way, sub, step],
            ahead if way == 0 else behind,
        )

    def mate_arrivals(m, step):
        for way in range(2):
            mate_copy(m, way, step).wait_recv()

    def sum_start(m):
        mate_arrivals(m, 0)
        for sub in range(SUBS):
            for way in range(2):
                owner, cols = owner_of(way, 0), cols_of(way, sub)
                acc[m, owner, core, :, cols] = acc[m, owner, core, :, cols] + mate[m, owner, :, cols]
                sum_copy(m, way, sub, 0, acc.at[m, owner, core, :, cols]).start()

    def sum_step(m, step):
        @pl.when(step < 4)
        def _():
            mate_arrivals(m, step)

        for sub in range(SUBS):
            for way in range(2):
                owner, cols = owner_of(way, step), cols_of(way, sub)
                held = slots.at[m, way, sub, step - 1]
                sum_copy(m, way, sub, step - 1, held).wait_recv()
                slots[m, way, sub, step - 1] = slots[m, way, sub, step - 1] + (
                    acc[m, owner, core, :, cols] + mate[m, owner, :, cols]
                )
                sum_copy(m, way, sub, step, held).start()

    nt = ff // TILE

    def fetch(m, t, buf):
        cols = pl.ds(pl.multiple_of(t * TILE, TILE), TILE)
        return pltpu.make_async_copy(wts.at[m, :, :, :, cols], tiles.at[m, buf], tile_sem.at[m, buf])

    def put_rows(k, i, value):
        high, low = split(value)
        to = pl.ds(i * 2 * quarter, 2 * quarter)
        right[k, to, :] = high
        right[k + 1, to, :] = low

    def factor_rows(i):
        here = pl.ds(i * 2 * quarter, 2 * quarter)
        copy = load(fa_ref.at[here], sa, 0)
        copy.start()
        copy.wait()
        put_rows(0, i, sa[...])

    def opened_rows(i):
        here = pl.ds(i * 2 * quarter, 2 * quarter)
        copies = [load(uo.at[here], sx, 0), load(ru.at[here], sx2, 1)]
        for copy in copies:
            copy.start()
        for copy in copies:
            copy.wait()
        put_rows(2, i, sx[...] + sx2[...])

    def first_tile(t):
        buf = lax.rem(t, 2)
        cols = pl.ds(pl.multiple_of(t * TILE, TILE), TILE)

        @pl.when(t + 1 < nt)
        def _():
            fetch(1, t + 1, 1 - buf).start()

        fetch(1, t, buf).wait()
        weight = split(tiles[1, buf].reshape(d, TILE))
        ybuf[:, cols] = ybuf[:, cols] + product((right[0], right[1]), weight)

    def second_tile(t):
        buf = lax.rem(t, 2)
        cols = pl.ds(pl.multiple_of(t * TILE, TILE), TILE)

        @pl.when(t + 1 < nt)
        def _():
            for m in range(2):
                fetch(m, t + 1, 1 - buf).start()

        for m in range(2):
            fetch(m, t, buf).wait()
        weight = split(tiles[0, buf].reshape(d, TILE) + keep * tiles[1, buf].reshape(d, TILE))
        ybuf[:, cols] = ybuf[:, cols] + product((right[2], right[3]), weight)

    second(0)
    sum_start(0)
    second(1)
    pass_on(1, steps - 1)
    late = 2 * steps - 6

    def several(tile, turn):
        def one(t, carry):
            tile(t)
            return carry

        lax.fori_loop(turn * nt // 3, (turn + 1) * nt // 3, one, 0)

    def drain_gather(step, carry):
        for m in range(2):
            for way in range(2):
                for sub in range(SUBS):
                    gather_copy(m, way, sub, step).wait_send()
        return carry

    def drain_early():
        lax.fori_loop(0, steps, drain_gather, 0)
        for m in range(2):
            for way in range(2):
                for k in range(4):
                    mate_copy(m, way, k).wait_send()
        mask_copy().wait_send()
        for side in range(2):

            @pl.when(party == side)
            def _():
                for j in range(2):
                    for copy in chunk_copies(side, j):
                        copy.wait_send()
        open_copy().wait_send()

    def forward(work):
        @pl.when(work == 3)
        def _():
            for m in range(2):
                pltpu.make_async_copy(wts.at[m, chip, core], wts.at[m, chip, core], lc_sem.at[m]).wait()
                everything = remote(wts.at[m, :, core], wts.at[m, :, 1 - core], ac_send.at[m], ac_recv.at[m], buddy)
                everything.wait_recv()
                everything.wait_send()
            fetch(1, 0, 0).start()
            fetch_y.wait()

        @pl.when(work == 4)
        def _():
            factor_rows(0)
            factor_rows(1)

        @pl.when(jnp.logical_and(work >= 5, work < 8))
        def _():
            several(first_tile, work - 5)

        @pl.when(jnp.logical_and(work > late, work <= late + 3))
        def _():
            several(second_tile, work - late - 1)

        @pl.when(work == late + 4)
        def _():
            drain_early()
            triple = load(bc_ref, got_w, 0)
            triple.start()
            triple.wait()

        @pl.when(work == late)
        def _():
            for m in range(2):
                fetch(m, 0, 0).start()
            open_copy().wait_recv()
            for i in range(2):
                opened_rows(i)

    def swap_copy(way, sub):
        cols = cols_of(way, sub)
        return remote(give.at[:, cols], got.at[:, cols], sw_send.at[way, sub], sw_recv.at[way, sub], other)

    def total(m, way, sub):
        cols = cols_of(way, sub)
        held = slots.at[m, way, sub, steps - 1]
        sum_copy(m, way, sub, steps - 1, held).wait_recv()
        return slots[m, way, sub, steps - 1] + (acc[m, chip, core, :, cols] + mate[m, chip, :, cols])

    def half_step(work, carry):
        m = lax.rem(work, 2)
        step = work // 2 + 1 - m
        forward(work)

        @pl.when(jnp.logical_and(m == 1, step < 2))
        def _():
            second(step + 2)

        @pl.when(step == 0)
        def _():
            sum_start(1)

        @pl.when(jnp.logical_and(step > 0, step < steps))
        def _():
            sum_step(m, step)

        @pl.when(step == steps)
        def _():
            for sub in range(SUBS):
                for way in range(2):
                    cols = cols_of(way, sub)
                    give[:, cols] = total(0, way, sub) - keep * got_w[:, cols]
                    swap_copy(way, sub).start()

        return carry

    lax.fori_loop(0, 2 * steps, half_step, 0)
    for sub in range(SUBS):
        for way in range(2):
            cols = cols_of(way, sub)
            dw_ref[:, cols] = total(1, way, sub) + keep * got_w[:, cols]
    for sub in range(SUBS):
        for way in range(2):
            cols = cols_of(way, sub)
            swap_copy(way, sub).wait_recv()
            dw_ref[:, cols] = dw_ref[:, cols] + got[:, cols]

    def drain(step, carry):
        for m in range(2):
            for way in range(2):
                for sub in range(SUBS):
                    sum_copy(m, way, sub, step, slots.at[m, way, sub, step]).wait_send()
        return carry

    lax.fori_loop(0, steps, drain, 0)
    for way in range(2):
        for sub in range(SUBS):
            swap_copy(way, sub).wait_send()


def body(n, x_share, w_share, g_share, fwd_a, fwd_b, fwd_c, bwd_a, bwd_b, bwd_c):
    tokens, d = x_share.shape[1:]
    rows, ff = fwd_b.shape[1:]
    nc = n // 2
    steps = nc - 1
    quarter, eighth = tokens // 4, tokens // 8
    piece = ff // (2 * SUBS)
    hbm = pl.BlockSpec(memory_space=pl.ANY)
    vmem = pl.BlockSpec(memory_space=pltpu.VMEM)
    dma = pltpu.SemaphoreType.DMA

    def shape(*dims):
        return jax.ShapeDtypeStruct(dims, F32)

    outs = pl.pallas_call(
        functools.partial(kernel, n),
        out_shape=[
            pltpu.VMEM((tokens, ff), F32),
            pltpu.VMEM((rows, ff), F32),
            shape(2, nc, 2, rows, ff),
            shape(tokens, d),
            shape(tokens, d),
            shape(tokens // 4, ff),
            shape(tokens, d),
            shape(tokens, d),
        ],
        in_specs=[hbm] * 9,
        out_specs=[vmem, vmem] + [hbm] * 6,
        scratch_shapes=[
            pltpu.VMEM((2, nc, 2, rows, ff), F32),
            pltpu.VMEM((2, nc, rows, ff), F32),
            pltpu.VMEM((2, 2, SUBS, steps, rows, piece), F32),
            pltpu.VMEM((3, 2, d, 2 * quarter), BF16),
            pltpu.VMEM((4, 4 * quarter, ff // 2), BF16),
            pltpu.VMEM((2 * quarter, d), F32),
            pltpu.VMEM((2 * quarter, d), F32),
            pltpu.VMEM((2 * quarter, d), F32),
            pltpu.VMEM((2 * quarter, d), F32),
            pltpu.VMEM((quarter, ff), F32),
            pltpu.VMEM((quarter, ff), F32),
            pltpu.VMEM((eighth, ff), F32),
            pltpu.VMEM((2, 2, nc, 2, rows, TILE), F32),
            pltpu.VMEM((rows, ff), F32),
            pltpu.VMEM((rows, ff), F32),
            pltpu.VMEM((rows, ff), F32),
            pltpu.VMEM((rows, ff), F32),
            pltpu.VMEM((rows, ff), F32),
            dma((7,)),
            dma((2, 2)),
            dma((2,)),
            dma((6,)),
            dma((6,)),
            dma((2, SUBS)),
            dma((2, SUBS)),
            dma((2, 2, SUBS, steps)),
            dma((2, 2, SUBS, steps)),
            dma((2,)),
            dma((2,)),
            dma((2, 2, SUBS, steps)),
            dma((2, 2, SUBS, steps)),
            dma((2, 2, 4)),
            dma((2, 2, 4)),
        ],
        compiler_params=pltpu.CompilerParams(collective_id=0, has_side_effects=True, vmem_limit_bytes=61_500_000),
        cost_estimate=pl.CostEstimate(flops=32 * tokens * d * ff, bytes_accessed=100 * 2**20, transcendentals=0),
    )(
        x_share[0],
        g_share[0],
        fwd_a[0],
        fwd_c[0],
        bwd_a[0],
        bwd_b[0],
        w_share[0],
        fwd_b[0],
        bwd_c[0],
    )
    return outs[0][None], outs[1][None]


def solution(mesh):
    spec = P("party", "dp", None)
    return jax.shard_map(
        functools.partial(body, mesh.shape["dp"]),
        mesh=mesh,
        in_specs=(spec,) * 9,
        out_specs=(spec, spec),
        check_vma=False,
    )
```

```python
import functools

import jax
import jax.numpy as jnp
from jax import lax
from jax.experimental import pallas as pl
from jax.experimental.pallas import tpu as pltpu
from jax.sharding import PartitionSpec as P

MESH = pl.DeviceIdType.MESH
BF16, F32 = jnp.bfloat16, jnp.float32
SUBS = 2
LAG = 2
TILE = 256
WIDE = 1024


def position(chip, nc):
    z, y = chip // 2, lax.rem(chip, 2)
    return z + y * (nc - 1 - 2 * z)


def chip_at(spot, nc):
    spot = lax.rem(spot + 2 * nc, nc)
    y = spot // (nc // 2)
    z = spot + y * (nc - 1 - 2 * spot)
    return 2 * z + y


def split(value):
    high = value.astype(BF16)
    return high, (value - high.astype(F32)).astype(BF16)


def product(left, right):
    def dot(a, b):
        return jnp.dot(a, b, preferred_element_type=F32)

    return dot(left[0], right[0]) + (dot(left[1], right[0]) + dot(left[0], right[1]))


def kernel(
    n,
    x_ref,
    g_ref,
    fa_ref,
    fc_ref,
    ba_ref,
    bb_ref,
    w_ref,
    fb_ref,
    bc_ref,
    ybuf,
    dw_ref,
    wts,
    rx,
    ra,
    rg,
    uo,
    ru,
    acc,
    mate,
    slots,
    lefts,
    right,
    sx,
    sx2,
    sa,
    sa2,
    sg,
    sb,
    sg2,
    vx,
    va,
    vg,
    tiles,
    own_w,
    got_w,
    delta,
    give,
    got,
    ld_sem,
    tile_sem,
    lc_sem,
    xs_send,
    xs_recv,
    sw_send,
    sw_recv,
    ag_send,
    ag_recv,
    ac_send,
    ac_recv,
    rs_send,
    rs_recv,
    mt_send,
    mt_recv,
):
    nc = n // 2
    steps = nc - 1
    party, me = lax.axis_index("party"), lax.axis_index("dp")
    core, chip = lax.rem(me, 2), me // 2
    spot = position(chip, nc)
    rows, ff = fb_ref.shape
    tokens, d = x_ref.shape
    quarter, eighth = tokens // 4, tokens // 8
    piece = ff // (2 * SUBS)
    first = party == 0
    other = {"party": 1 - party}
    buddy = {"dp": me + 1 - 2 * core}
    ahead = {"dp": 2 * chip_at(spot + 1, nc) + core}
    behind = {"dp": 2 * chip_at(spot - 1, nc) + core}

    def cols_of(way, sub):
        return pl.ds((way * SUBS + sub) * piece, piece)

    def half_of(way):
        return pl.ds(way * (ff // 2), ff // 2)

    def remote(src, dst, send, recv, device):
        return pltpu.make_async_remote_copy(
            src_ref=src, dst_ref=dst, send_sem=send, recv_sem=recv, device_id=device, device_id_type=MESH
        )

    masks = [pltpu.make_async_copy(w_ref, own_w, ld_sem.at[0]), pltpu.make_async_copy(fb_ref, delta, ld_sem.at[1])]
    for copy in masks:
        copy.start()
    barrier = pltpu.get_barrier_semaphore()
    for device in (other, buddy, ahead, behind):
        pl.semaphore_signal(barrier, inc=1, device_id=device, device_id_type=MESH)
    pl.semaphore_wait(barrier, 4)

    def chunk_copies(side, j):
        start = j * 2 * quarter
        k = 1 + 2 * j
        if side == 0:
            everything = pl.ds(start, 2 * quarter)
            tail = pl.ds(start + 3 * eighth, eighth)
            to_x = rx.at[everything] if j == 0 else vx
            to_g = rg if j == 0 else vg
            return [
                remote(x_ref.at[everything], to_x, xs_send.at[k], xs_recv.at[k], other),
                remote(g_ref.at[tail], to_g, xs_send.at[k + 1], xs_recv.at[k + 1], other),
            ]
        head = pl.ds(start, 3 * eighth)
        local = pl.ds(0, 3 * eighth)
        to_x, to_a = (rx.at[head], ra.at[head]) if j == 0 else (vx.at[local], va.at[local])
        return [
            remote(x_ref.at[head], to_x, xs_send.at[k], xs_recv.at[k], other),
            remote(ba_ref.at[head], to_a, xs_send.at[k + 1], xs_recv.at[k + 1], other),
        ]

    def mask_copy():
        return remote(own_w, got_w, xs_send.at[0], xs_recv.at[0], other)

    def open_copy():
        return remote(uo, ru, xs_send.at[5], xs_recv.at[5], other)

    def gather_copy(m, way, sub, step):
        owner = chip_at(spot - step, nc) if way == 0 else chip_at(spot + step, nc)
        return remote(
            wts.at[m, owner, core, :, cols_of(way, sub)],
            wts.at[m, owner, core, :, cols_of(way, sub)],
            ag_send.at[m, way, sub, step],
            ag_recv.at[m, way, sub, step],
            ahead if way == 0 else behind,
        )

    def gather_first(m, way, sub, source):
        return remote(
            source.at[:, cols_of(way, sub)],
            wts.at[m, chip, core, :, cols_of(way, sub)],
            ag_send.at[m, way, sub, 0],
            ag_recv.at[m, way, sub, 0],
            ahead if way == 0 else behind,
        )

    def gather_arrival(m, way, sub, step):
        owner = chip_at(spot - 1 - step, nc) if way == 0 else chip_at(spot + 1 + step, nc)
        here = wts.at[m, owner, core, :, cols_of(way, sub)]
        return remote(here, here, ag_send.at[m, way, sub, step], ag_recv.at[m, way, sub, step], ahead)

    def begin_gather(m, source):
        for sub in range(SUBS):
            for way in range(2):
                gather_first(m, way, sub, source).start()
        remote(source, wts.at[m, chip, core], ac_send.at[m], ac_recv.at[m], buddy).start()
        pltpu.make_async_copy(source, wts.at[m, chip, core], lc_sem.at[m]).start()

    def pass_on(m, step):
        for sub in range(SUBS):
            for way in range(2):
                gather_arrival(m, way, sub, step).wait_recv()

                @pl.when(step < steps - 1)
                def _():
                    gather_copy(m, way, sub, step + 1).start()

        for way in range(2):
            owner = chip_at(spot - 1 - step, nc) if way == 0 else chip_at(spot + 1 + step, nc)
            here = wts.at[m, owner, core, :, half_of(way)]
            remote(here, here, ac_send.at[m], ac_recv.at[m], buddy).start()

    def load(src, dst, k):
        return pltpu.make_async_copy(src, dst, ld_sem.at[k])

    def open_rows(i):
        part = pl.ds(pl.multiple_of(i * quarter, 8), quarter)
        at = pl.ds(0, quarter)
        copies = [load(x_ref.at[part], sx.at[at], 0), load(fa_ref.at[part], sa.at[at], 1)]
        for copy in copies:
            copy.start()
        for copy in copies:
            copy.wait()
        sx2[:quarter, :] = sx[:quarter, :] - sa[:quarter, :]
        out = load(sx2.at[at], uo.at[part], 2)
        out.start()
        out.wait()

    def put_left(k, at, value):
        high, low = split(value)
        lefts[k, 0, :, at] = high.T
        lefts[k, 1, :, at] = low.T

    def put_right(k, at, value):
        high, low = split(value)
        for half in range(2):
            to = slice(half * 2 * quarter + at.start, half * 2 * quarter + at.stop)
            right[2 * k, to, :] = high[:, half * (ff // 2) : (half + 1) * (ff // 2)]
            right[2 * k + 1, to, :] = low[:, half * (ff // 2) : (half + 1) * (ff // 2)]

    def owned(j):
        start = 2 * j * quarter
        both = pl.ds(start, 2 * quarter)
        rest = [load(x_ref.at[both], sx, 0), load(ba_ref.at[both], sa, 1)]
        for copy in rest:
            copy.start()
        for part in range(2):
            here = pl.ds(start + part * quarter, quarter)
            to = slice(part * quarter, (part + 1) * quarter)
            own = [load(g_ref.at[here], sg, 2), load(bb_ref.at[here], sb, 3)]
            for copy in own:
                copy.start()
            for copy in own:
                copy.wait()
            put_right(1, to, sb[...])

            @pl.when(first)
            def _():
                if part == 1:
                    sg[eighth:, :] = jnp.zeros((eighth, ff), F32)
                put_right(0, to, sg[...])

            @pl.when(jnp.logical_not(first))
            def _():
                sg[...] = sg[...] - sb[...]
                put_right(0, to, sg[...])

        for copy in rest:
            copy.wait()
        whole = slice(0, 2 * quarter)

        @pl.when(first)
        def _():
            put_left(2, whole, sa[...])

        @pl.when(jnp.logical_not(first))
        def _():
            put_left(1, whole, sa[...])

    def received(j):
        start = 2 * j * quarter
        whole = slice(0, 2 * quarter)
        many = 3 * eighth
        in_x, in_a, in_g = (sx2, sa2, sg2) if j == 0 else (vx, va, vg)

        def fetch_all(copies):
            if j == 0:
                for copy in copies:
                    copy.start()
                for copy in copies:
                    copy.wait()

        @pl.when(first)
        def _():
            for copy in chunk_copies(1, j):
                copy.wait_recv()
            if j == 0:
                some, local = pl.ds(start, many), pl.ds(0, many)
                fetch_all([load(rx.at[some], sx2.at[local], 4), load(ra.at[some], sa2.at[local], 5)])
            in_x[many:, :] = jnp.zeros((eighth, d), F32)
            in_a[many:, :] = jnp.zeros((eighth, d), F32)
            sx[many:, :] = jnp.zeros((eighth, d), F32)
            put_left(0, whole, in_a[...])
            put_left(1, whole, (sx[...] + in_x[...]) - in_a[...])

        @pl.when(jnp.logical_not(first))
        def _():
            for copy in chunk_copies(0, j):
                copy.wait_recv()
            if j == 0:
                fetch_all([load(rx.at[pl.ds(start, 2 * quarter)], sx2, 4), load(rg, sg2, 5)])
            put_right(0, slice(many, 2 * quarter), sg[eighth:, :] + in_g[...])
            sx[...] = sx[...] + in_x[...]
            put_left(0, whole, sx[...] - sa[...])
            put_left(2, whole, sx[...])

    keep = jnp.where(first, 1.0, 0.0).astype(F32)
    sign = 1.0 - 2.0 * keep
    group = d // 4
    per = group // (2 * rows)

    def gradient_rows(j, q, tile_from, tile_to, only=None):
        at = pl.ds(pl.multiple_of(q * group, group), group)
        chips = pl.ds(q * per, per)

        def tile(t, carry):
            half = t // (ff // 2 // WIDE)
            deep = pl.ds(pl.multiple_of(half * 2 * quarter, 2 * quarter), 2 * quarter)
            wide = pl.ds(pl.multiple_of(lax.rem(t, ff // 2 // WIDE) * WIDE, WIDE), WIDE)
            cols = pl.ds(pl.multiple_of(t * WIDE, WIDE), WIDE)

            def multiply(k, m):
                return product(
                    (lefts[k, 0, at, :], lefts[k, 1, at, :]),
                    (right[2 * m, deep, wide], right[2 * m + 1, deep, wide]),
                )

            shared = multiply(2, 1)
            shape = (per, 2, rows, WIDE)
            for m in range(2):
                if only is None or only == m:
                    value = (multiply(m, 0) + (sign if m else keep) * shared).reshape(shape)
                    if j == 1:
                        value = acc[m, chips, :, :, cols] + value
                    acc[m, chips, :, :, cols] = value
            return carry

        lax.fori_loop(tile_from, tile_to, tile, 0)

    begin_gather(0, fb_ref)
    for copy in masks:
        copy.wait()
    own_w[...] = own_w[...] - delta[...]
    mask_copy().start()
    for side in range(2):

        @pl.when(party == side)
        def _():
            for j in range(2):
                for copy in chunk_copies(side, j):
                    copy.start()

    early = steps - 3

    def gather_step(i, carry):
        @pl.when(i < steps)
        def _():
            pass_on(0, i)

        @pl.when(i < 4)
        def _():
            open_rows(i)

        @pl.when(i == 3)
        def _():
            open_copy().start()

        @pl.when(i == early)
        def _():
            owned(0)
            received(0)

        @pl.when(i > early)
        def _():
            @pl.when(i <= early + 2)
            def _():
                gradient_rows(0, 2 * (i - early - 1), 0, ff // WIDE)

        @pl.when(i == LAG - 1)
        def _():
            mask_copy().wait_recv()
            delta[...] = own_w[...] + got_w[...]
            begin_gather(1, delta)

        @pl.when(i >= LAG)
        def _():
            pass_on(1, i - LAG)

        @pl.when(i > early)
        def _():
            @pl.when(i <= early + 2)
            def _():
                gradient_rows(0, 2 * (i - early - 1) + 1, 0, ff // WIDE)

        @pl.when(i == early + 2)
        def _():
            owned(1)

        return carry

    lax.fori_loop(0, steps + LAG - 1, gather_step, 0)

    received(1)
    zs, span = nc // 2, nc // 8

    def group_at(way, k):
        place = jnp.where(way == 0, spot, nc - 1 - spot)
        falling = (place + span - 1) // span
        rising = (nc - place) // span
        low = jnp.where(k < falling, falling - 1 - k, k)
        high = jnp.where(k < 4 - rising, rising + k, 3 - k)
        return jnp.where(place <= zs, low, high)

    def mate_copy(m, way, k):
        chips = pl.ds(group_at(way, k) * per, per)
        cols = pl.ds(pl.multiple_of(way * (ff // 2), 128), ff // 2)
        return remote(
            acc.at[m, chips, 1 - core, :, cols],
            mate.at[m, chips, :, cols],
            mt_send.at[m, way, k],
            mt_recv.at[m, way, k],
            buddy,
        )

    def second(k):
        def one(way, carry):
            gradient_rows(1, group_at(way, k), way * (ff // 2 // WIDE), (way + 1) * (ff // 2 // WIDE))
            for m in range(2):
                mate_copy(m, way, k).start()
            return carry

        lax.fori_loop(0, 2, one, 0)

    fetch_y = load(fc_ref, ybuf, 6)
    fetch_y.start()

    def owner_of(way, step):
        return chip_at(spot - 1 - step, nc) if way == 0 else chip_at(spot + 1 + step, nc)

    def sum_copy(m, way, sub, step, source):
        return remote(
            source,
            slots.at[m, way, sub, step],
            rs_send.at[m, way, sub, step],
            rs_recv.at[m, way, sub, step],
            ahead if way == 0 else behind,
        )

    def mate_arrivals(m, step):
        for way in range(2):
            mate_copy(m, way, step).wait_recv()

    def sum_start(m):
        for way in range(2):
            mate_copy(m, way, 0).wait_recv()
            for sub in range(SUBS):
                owner, cols = owner_of(way, 0), cols_of(way, sub)
                acc[m, owner, core, :, cols] = acc[m, owner, core, :, cols] + mate[m, owner, :, cols]
                sum_copy(m, way, sub, 0, acc.at[m, owner, core, :, cols]).start()

    def sum_step(m, step):
        @pl.when(step < 4)
        def _():
            mate_arrivals(m, step)

        for sub in range(SUBS):
            for way in range(2):
                owner, cols = owner_of(way, step), cols_of(way, sub)
                held = slots.at[m, way, sub, step - 1]
                sum_copy(m, way, sub, step - 1, held).wait_recv()
                slots[m, way, sub, step - 1] = slots[m, way, sub, step - 1] + (
                    acc[m, owner, core, :, cols] + mate[m, owner, :, cols]
                )
                sum_copy(m, way, sub, step, held).start()

    nt = ff // TILE

    def fetch(m, t, buf):
        cols = pl.ds(pl.multiple_of(t * TILE, TILE), TILE)
        return pltpu.make_async_copy(wts.at[m, :, :, :, cols], tiles.at[m, buf], tile_sem.at[m, buf])

    def put_rows(k, i, value):
        high, low = split(value)
        to = pl.ds(i * 2 * quarter, 2 * quarter)
        right[k, to, :] = high
        right[k + 1, to, :] = low

    def factor_rows(i):
        here = pl.ds(i * 2 * quarter, 2 * quarter)
        copy = load(fa_ref.at[here], sa, 0)
        copy.start()
        copy.wait()
        put_rows(0, i, sa[...])

    def opened_rows(i):
        here = pl.ds(i * 2 * quarter, 2 * quarter)
        copies = [load(uo.at[here], sx, 0), load(ru.at[here], sx2, 1)]
        for copy in copies:
            copy.start()
        for copy in copies:
            copy.wait()
        put_rows(2, i, sx[...] + sx2[...])

    def first_tile(t):
        buf = lax.rem(t, 2)
        cols = pl.ds(pl.multiple_of(t * TILE, TILE), TILE)

        @pl.when(t + 1 < nt)
        def _():
            fetch(1, t + 1, 1 - buf).start()

        fetch(1, t, buf).wait()
        weight = split(tiles[1, buf].reshape(d, TILE))
        ybuf[:, cols] = ybuf[:, cols] + product((right[0], right[1]), weight)

    def second_tile(t):
        buf = lax.rem(t, 2)
        cols = pl.ds(pl.multiple_of(t * TILE, TILE), TILE)

        @pl.when(t + 1 < nt)
        def _():
            for m in range(2):
                fetch(m, t + 1, 1 - buf).start()

        for m in range(2):
            fetch(m, t, buf).wait()
        weight = split(tiles[0, buf].reshape(d, TILE) + keep * tiles[1, buf].reshape(d, TILE))
        ybuf[:, cols] = ybuf[:, cols] + product((right[2], right[3]), weight)

    for m in range(2):

        def opening(way, carry):
            gradient_rows(1, group_at(way, 0), way * (ff // 2 // WIDE), (way + 1) * (ff // 2 // WIDE), m)
            mate_copy(m, way, 0).start()
            return carry

        lax.fori_loop(0, 2, opening, 0)
        if m == 0:
            sum_start(0)
    second(1)
    pass_on(1, steps - 1)
    late = 2 * steps - 6

    def several(tile, turn):
        def one(t, carry):
            tile(t)
            return carry

        lax.fori_loop(turn * nt // 3, (turn + 1) * nt // 3, one, 0)

    def drain_gather(step, carry):
        for m in range(2):
            for way in range(2):
                for sub in range(SUBS):
                    gather_copy(m, way, sub, step).wait_send()
        return carry

    def drain_early():
        lax.fori_loop(0, steps, drain_gather, 0)
        for m in range(2):
            for way in range(2):
                for k in range(4):
                    mate_copy(m, way, k).wait_send()
        mask_copy().wait_send()
        for side in range(2):

            @pl.when(party == side)
            def _():
                for j in range(2):
                    for copy in chunk_copies(side, j):
                        copy.wait_send()
        open_copy().wait_send()

    def forward(work):
        @pl.when(work == 3)
        def _():
            for m in range(2):
                pltpu.make_async_copy(wts.at[m, chip, core], wts.at[m, chip, core], lc_sem.at[m]).wait()
                everything = remote(wts.at[m, :, core], wts.at[m, :, 1 - core], ac_send.at[m], ac_recv.at[m], buddy)
                everything.wait_recv()
                everything.wait_send()
            fetch(1, 0, 0).start()
            fetch_y.wait()

        @pl.when(work == 4)
        def _():
            factor_rows(0)
            factor_rows(1)

        @pl.when(jnp.logical_and(work >= 5, work < 8))
        def _():
            several(first_tile, work - 5)

        @pl.when(jnp.logical_and(work > late, work <= late + 3))
        def _():
            several(second_tile, work - late - 1)

        @pl.when(work == late + 4)
        def _():
            drain_early()
            triple = load(bc_ref, got_w, 0)
            triple.start()
            triple.wait()

        @pl.when(work == late)
        def _():
            for m in range(2):
                fetch(m, 0, 0).start()
            open_copy().wait_recv()
            for i in range(2):
                opened_rows(i)

    def swap_copy(way, sub):
        cols = cols_of(way, sub)
        return remote(give.at[:, cols], got.at[:, cols], sw_send.at[way, sub], sw_recv.at[way, sub], other)

    def total(m, way, sub):
        cols = cols_of(way, sub)
        held = slots.at[m, way, sub, steps - 1]
        sum_copy(m, way, sub, steps - 1, held).wait_recv()
        return slots[m, way, sub, steps - 1] + (acc[m, chip, core, :, cols] + mate[m, chip, :, cols])

    def half_step(work, carry):
        m = lax.rem(work, 2)
        step = work // 2 + 1 - m
        forward(work)

        @pl.when(jnp.logical_and(m == 1, step < 2))
        def _():
            second(step + 2)

        @pl.when(step == 0)
        def _():
            sum_start(1)

        @pl.when(jnp.logical_and(step > 0, step < steps))
        def _():
            sum_step(m, step)

        @pl.when(step == steps)
        def _():
            for sub in range(SUBS):
                for way in range(2):
                    cols = cols_of(way, sub)
                    give[:, cols] = total(0, way, sub) - keep * got_w[:, cols]
                    swap_copy(way, sub).start()

        return carry

    lax.fori_loop(0, 2 * steps, half_step, 0)
    for sub in range(SUBS):
        for way in range(2):
            cols = cols_of(way, sub)
            dw_ref[:, cols] = total(1, way, sub) + keep * got_w[:, cols]
    for sub in range(SUBS):
        for way in range(2):
            cols = cols_of(way, sub)
            swap_copy(way, sub).wait_recv()
            dw_ref[:, cols] = dw_ref[:, cols] + got[:, cols]

    def drain(step, carry):
        for m in range(2):
            for way in range(2):
                for sub in range(SUBS):
                    sum_copy(m, way, sub, step, slots.at[m, way, sub, step]).wait_send()
        return carry

    lax.fori_loop(0, steps, drain, 0)
    for way in range(2):
        for sub in range(SUBS):
            swap_copy(way, sub).wait_send()


def body(n, x_share, w_share, g_share, fwd_a, fwd_b, fwd_c, bwd_a, bwd_b, bwd_c):
    tokens, d = x_share.shape[1:]
    rows, ff = fwd_b.shape[1:]
    nc = n // 2
    steps = nc - 1
    quarter, eighth = tokens // 4, tokens // 8
    piece = ff // (2 * SUBS)
    hbm = pl.BlockSpec(memory_space=pl.ANY)
    vmem = pl.BlockSpec(memory_space=pltpu.VMEM)
    dma = pltpu.SemaphoreType.DMA

    def shape(*dims):
        return jax.ShapeDtypeStruct(dims, F32)

    outs = pl.pallas_call(
        functools.partial(kernel, n),
        out_shape=[
            pltpu.VMEM((tokens, ff), F32),
            pltpu.VMEM((rows, ff), F32),
            shape(2, nc, 2, rows, ff),
            shape(tokens // 2, d),
            shape(tokens // 2, d),
            shape(tokens // 8, ff),
            shape(tokens, d),
            shape(tokens, d),
        ],
        in_specs=[hbm] * 9,
        out_specs=[vmem, vmem] + [hbm] * 6,
        scratch_shapes=[
            pltpu.VMEM((2, nc, 2, rows, ff), F32),
            pltpu.VMEM((2, nc, rows, ff), F32),
            pltpu.VMEM((2, 2, SUBS, steps, rows, piece), F32),
            pltpu.VMEM((3, 2, d, 2 * quarter), BF16),
            pltpu.VMEM((4, 4 * quarter, ff // 2), BF16),
            pltpu.VMEM((2 * quarter, d), F32),
            pltpu.VMEM((2 * quarter, d), F32),
            pltpu.VMEM((2 * quarter, d), F32),
            pltpu.VMEM((2 * quarter, d), F32),
            pltpu.VMEM((quarter, ff), F32),
            pltpu.VMEM((quarter, ff), F32),
            pltpu.VMEM((eighth, ff), F32),
            pltpu.VMEM((2 * quarter, d), F32),
            pltpu.VMEM((2 * quarter, d), F32),
            pltpu.VMEM((eighth, ff), F32),
            pltpu.VMEM((2, 2, nc, 2, rows, TILE), F32),
            pltpu.VMEM((rows, ff), F32),
            pltpu.VMEM((rows, ff), F32),
            pltpu.VMEM((rows, ff), F32),
            pltpu.VMEM((rows, ff), F32),
            pltpu.VMEM((rows, ff), F32),
            dma((7,)),
            dma((2, 2)),
            dma((2,)),
            dma((6,)),
            dma((6,)),
            dma((2, SUBS)),
            dma((2, SUBS)),
            dma((2, 2, SUBS, steps)),
            dma((2, 2, SUBS, steps)),
            dma((2,)),
            dma((2,)),
            dma((2, 2, SUBS, steps)),
            dma((2, 2, SUBS, steps)),
            dma((2, 2, 4)),
            dma((2, 2, 4)),
        ],
        compiler_params=pltpu.CompilerParams(collective_id=0, has_side_effects=True, vmem_limit_bytes=61_500_000),
        cost_estimate=pl.CostEstimate(flops=32 * tokens * d * ff, bytes_accessed=100 * 2**20, transcendentals=0),
    )(
        x_share[0],
        g_share[0],
        fwd_a[0],
        fwd_c[0],
        bwd_a[0],
        bwd_b[0],
        w_share[0],
        fwd_b[0],
        bwd_c[0],
    )
    return outs[0][None], outs[1][None]


def solution(mesh):
    spec = P("party", "dp", None)
    return jax.shard_map(
        functools.partial(body, mesh.shape["dp"]),
        mesh=mesh,
        in_specs=(spec,) * 9,
        out_specs=(spec, spec),
        check_vma=False,
    )
```

```python
import functools

import jax
import jax.numpy as jnp
from jax import lax
from jax.experimental import pallas as pl
from jax.experimental.pallas import tpu as pltpu
from jax.sharding import PartitionSpec as P

MESH = pl.DeviceIdType.MESH
BF16, F32 = jnp.bfloat16, jnp.float32
SUBS = 2
LAG = 2
TILE = 256
WIDE = 1024


def position(chip, nc):
    z, y = chip // 2, lax.rem(chip, 2)
    return z + y * (nc - 1 - 2 * z)


def chip_at(spot, nc):
    spot = lax.rem(spot + 2 * nc, nc)
    y = spot // (nc // 2)
    z = spot + y * (nc - 1 - 2 * spot)
    return 2 * z + y


def split(value):
    high = value.astype(BF16)
    return high, (value - high.astype(F32)).astype(BF16)


def product(left, right):
    def dot(a, b):
        return jnp.dot(a, b, preferred_element_type=F32)

    return dot(left[0], right[0]) + (dot(left[1], right[0]) + dot(left[0], right[1]))


def kernel(
    n,
    x_ref,
    g_ref,
    fa_ref,
    fc_ref,
    ba_ref,
    bb_ref,
    w_ref,
    fb_ref,
    bc_ref,
    ybuf,
    dw_ref,
    wts,
    rx,
    ra,
    rg,
    uo,
    ru,
    acc,
    mate,
    slots,
    lefts,
    right,
    sx,
    sx2,
    sa,
    sa2,
    sg,
    sb,
    sg2,
    vx,
    va,
    vg,
    tiles,
    own_w,
    got_w,
    delta,
    give,
    got,
    ld_sem,
    tile_sem,
    lc_sem,
    xs_send,
    xs_recv,
    sw_send,
    sw_recv,
    ag_send,
    ag_recv,
    ac_send,
    ac_recv,
    rs_send,
    rs_recv,
    mt_send,
    mt_recv,
):
    nc = n // 2
    steps = nc - 1
    party, me = lax.axis_index("party"), lax.axis_index("dp")
    core, chip = lax.rem(me, 2), me // 2
    spot = position(chip, nc)
    rows, ff = fb_ref.shape
    tokens, d = x_ref.shape
    quarter, eighth = tokens // 4, tokens // 8
    piece = ff // (2 * SUBS)
    first = party == 0
    other = {"party": 1 - party}
    buddy = {"dp": me + 1 - 2 * core}
    ahead = {"dp": 2 * chip_at(spot + 1, nc) + core}
    behind = {"dp": 2 * chip_at(spot - 1, nc) + core}

    def cols_of(way, sub):
        return pl.ds((way * SUBS + sub) * piece, piece)

    def half_of(way):
        return pl.ds(way * (ff // 2), ff // 2)

    def remote(src, dst, send, recv, device):
        return pltpu.make_async_remote_copy(
            src_ref=src, dst_ref=dst, send_sem=send, recv_sem=recv, device_id=device, device_id_type=MESH
        )

    masks = [pltpu.make_async_copy(w_ref, own_w, ld_sem.at[0]), pltpu.make_async_copy(fb_ref, delta, ld_sem.at[1])]
    for copy in masks:
        copy.start()
    barrier = pltpu.get_barrier_semaphore()
    for device in (other, buddy, ahead, behind):
        pl.semaphore_signal(barrier, inc=1, device_id=device, device_id_type=MESH)
    pl.semaphore_wait(barrier, 4)

    def chunk_copies(side, j):
        start = j * 2 * quarter
        k = 1 + 2 * j
        if side == 0:
            everything = pl.ds(start, 2 * quarter)
            tail = pl.ds(start + 3 * eighth, eighth)
            to_x = rx.at[everything] if j == 0 else vx
            to_g = rg if j == 0 else vg
            return [
                remote(x_ref.at[everything], to_x, xs_send.at[k], xs_recv.at[k], other),
                remote(g_ref.at[tail], to_g, xs_send.at[k + 1], xs_recv.at[k + 1], other),
            ]
        head = pl.ds(start, 3 * eighth)
        local = pl.ds(0, 3 * eighth)
        to_x, to_a = (rx.at[head], ra.at[head]) if j == 0 else (vx.at[local], va.at[local])
        return [
            remote(x_ref.at[head], to_x, xs_send.at[k], xs_recv.at[k], other),
            remote(ba_ref.at[head], to_a, xs_send.at[k + 1], xs_recv.at[k + 1], other),
        ]

    def mask_copy():
        return remote(own_w, got_w, xs_send.at[0], xs_recv.at[0], other)

    def open_copy():
        return remote(uo, ru, xs_send.at[5], xs_recv.at[5], other)

    def gather_copy(m, way, sub, step):
        owner = chip_at(spot - step, nc) if way == 0 else chip_at(spot + step, nc)
        return remote(
            wts.at[m, owner, core, :, cols_of(way, sub)],
            wts.at[m, owner, core, :, cols_of(way, sub)],
            ag_send.at[m, way, sub, step],
            ag_recv.at[m, way, sub, step],
            ahead if way == 0 else behind,
        )

    def gather_first(m, way, sub, source):
        return remote(
            source.at[:, cols_of(way, sub)],
            wts.at[m, chip, core, :, cols_of(way, sub)],
            ag_send.at[m, way, sub, 0],
            ag_recv.at[m, way, sub, 0],
            ahead if way == 0 else behind,
        )

    def gather_arrival(m, way, sub, step):
        owner = chip_at(spot - 1 - step, nc) if way == 0 else chip_at(spot + 1 + step, nc)
        here = wts.at[m, owner, core, :, cols_of(way, sub)]
        return remote(here, here, ag_send.at[m, way, sub, step], ag_recv.at[m, way, sub, step], ahead)

    def begin_gather(m, source):
        for sub in range(SUBS):
            for way in range(2):
                gather_first(m, way, sub, source).start()
        remote(source, wts.at[m, chip, core], ac_send.at[m], ac_recv.at[m], buddy).start()
        pltpu.make_async_copy(source, wts.at[m, chip, core], lc_sem.at[m]).start()

    def pass_on(m, step):
        for sub in range(SUBS):
            for way in range(2):
                gather_arrival(m, way, sub, step).wait_recv()

                @pl.when(step < steps - 1)
                def _():
                    gather_copy(m, way, sub, step + 1).start()

        for way in range(2):
            owner = chip_at(spot - 1 - step, nc) if way == 0 else chip_at(spot + 1 + step, nc)
            here = wts.at[m, owner, core, :, half_of(way)]
            remote(here, here, ac_send.at[m], ac_recv.at[m], buddy).start()

    def load(src, dst, k):
        return pltpu.make_async_copy(src, dst, ld_sem.at[k])

    def open_rows(i):
        part = pl.ds(pl.multiple_of(i * quarter, 8), quarter)
        at = pl.ds(0, quarter)
        copies = [load(x_ref.at[part], sx.at[at], 0), load(fa_ref.at[part], sa.at[at], 1)]
        for copy in copies:
            copy.start()
        for copy in copies:
            copy.wait()
        sx2[:quarter, :] = sx[:quarter, :] - sa[:quarter, :]
        out = load(sx2.at[at], uo.at[part], 2)
        out.start()
        out.wait()

    def put_left(k, at, value):
        high, low = split(value)
        lefts[k, 0, :, at] = high.T
        lefts[k, 1, :, at] = low.T

    def put_right(k, at, value):
        high, low = split(value)
        for half in range(2):
            to = slice(half * 2 * quarter + at.start, half * 2 * quarter + at.stop)
            right[2 * k, to, :] = high[:, half * (ff // 2) : (half + 1) * (ff // 2)]
            right[2 * k + 1, to, :] = low[:, half * (ff // 2) : (half + 1) * (ff // 2)]

    def owned(j):
        start = 2 * j * quarter
        both = pl.ds(start, 2 * quarter)
        rest = [load(x_ref.at[both], sx, 0), load(ba_ref.at[both], sa, 1)]
        for copy in rest:
            copy.start()
        for part in range(2):
            here = pl.ds(start + part * quarter, quarter)
            to = slice(part * quarter, (part + 1) * quarter)
            own = [load(g_ref.at[here], sg, 2), load(bb_ref.at[here], sb, 3)]
            for copy in own:
                copy.start()
            for copy in own:
                copy.wait()
            put_right(1, to, sb[...])

            @pl.when(first)
            def _():
                if part == 1:
                    sg[eighth:, :] = jnp.zeros((eighth, ff), F32)
                put_right(0, to, sg[...])

            @pl.when(jnp.logical_not(first))
            def _():
                sg[...] = sg[...] - sb[...]
                put_right(0, to, sg[...])

        for copy in rest:
            copy.wait()
        whole = slice(0, 2 * quarter)

        @pl.when(first)
        def _():
            put_left(2, whole, sa[...])

        @pl.when(jnp.logical_not(first))
        def _():
            put_left(1, whole, sa[...])

    def received(j):
        start = 2 * j * quarter
        whole = slice(0, 2 * quarter)
        many = 3 * eighth
        in_x, in_a, in_g = (sx2, sa2, sg2) if j == 0 else (vx, va, vg)

        def fetch_all(copies):
            if j == 0:
                for copy in copies:
                    copy.start()
                for copy in copies:
                    copy.wait()

        @pl.when(first)
        def _():
            for copy in chunk_copies(1, j):
                copy.wait_recv()
            if j == 0:
                some, local = pl.ds(start, many), pl.ds(0, many)
                fetch_all([load(rx.at[some], sx2.at[local], 4), load(ra.at[some], sa2.at[local], 5)])
            in_x[many:, :] = jnp.zeros((eighth, d), F32)
            in_a[many:, :] = jnp.zeros((eighth, d), F32)
            sx[many:, :] = jnp.zeros((eighth, d), F32)
            put_left(0, whole, in_a[...])
            put_left(1, whole, (sx[...] + in_x[...]) - in_a[...])

        @pl.when(jnp.logical_not(first))
        def _():
            for copy in chunk_copies(0, j):
                copy.wait_recv()
            if j == 0:
                fetch_all([load(rx.at[pl.ds(start, 2 * quarter)], sx2, 4), load(rg, sg2, 5)])
            put_right(0, slice(many, 2 * quarter), sg[eighth:, :] + in_g[...])
            sx[...] = sx[...] + in_x[...]
            put_left(0, whole, sx[...] - sa[...])
            put_left(2, whole, sx[...])

    keep = jnp.where(first, 1.0, 0.0).astype(F32)
    sign = 1.0 - 2.0 * keep
    group = d // 4
    per = group // (2 * rows)

    def gradient_rows(j, q, tile_from, tile_to, only=None):
        at = pl.ds(pl.multiple_of(q * group, group), group)
        chips = pl.ds(q * per, per)

        def tile(t, carry):
            half = t // (ff // 2 // WIDE)
            deep = pl.ds(pl.multiple_of(half * 2 * quarter, 2 * quarter), 2 * quarter)
            wide = pl.ds(pl.multiple_of(lax.rem(t, ff // 2 // WIDE) * WIDE, WIDE), WIDE)
            cols = pl.ds(pl.multiple_of(t * WIDE, WIDE), WIDE)

            def multiply(k, m):
                return product(
                    (lefts[k, 0, at, :], lefts[k, 1, at, :]),
                    (right[2 * m, deep, wide], right[2 * m + 1, deep, wide]),
                )

            shared = multiply(2, 1)
            shape = (per, 2, rows, WIDE)
            for m in range(2):
                if only is None or only == m:
                    value = (multiply(m, 0) + (sign if m else keep) * shared).reshape(shape)
                    if j == 1:
                        value = acc[m, chips, :, :, cols] + value
                    acc[m, chips, :, :, cols] = value
            return carry

        lax.fori_loop(tile_from, tile_to, tile, 0)

    begin_gather(0, fb_ref)
    for copy in masks:
        copy.wait()
    own_w[...] = own_w[...] - delta[...]
    mask_copy().start()
    for side in range(2):

        @pl.when(party == side)
        def _():
            for j in range(2):
                for copy in chunk_copies(side, j):
                    copy.start()

    early = steps - 3

    def gather_step(i, carry):
        @pl.when(i < steps)
        def _():
            pass_on(0, i)

        @pl.when(i < 4)
        def _():
            open_rows(i)

        @pl.when(i == 3)
        def _():
            open_copy().start()

        @pl.when(i == early)
        def _():
            owned(0)
            received(0)

        @pl.when(i > early)
        def _():
            @pl.when(i <= early + 2)
            def _():
                gradient_rows(0, 2 * (i - early - 1), 0, ff // WIDE)

        @pl.when(i == LAG - 1)
        def _():
            mask_copy().wait_recv()
            delta[...] = own_w[...] + got_w[...]
            begin_gather(1, delta)

        @pl.when(i >= LAG)
        def _():
            pass_on(1, i - LAG)

        @pl.when(i > early)
        def _():
            @pl.when(i <= early + 2)
            def _():
                gradient_rows(0, 2 * (i - early - 1) + 1, 0, ff // WIDE)

        @pl.when(i == early + 2)
        def _():
            owned(1)

        return carry

    lax.fori_loop(0, steps + LAG - 1, gather_step, 0)

    received(1)
    zs, span = nc // 2, nc // 8

    def group_at(way, k):
        place = jnp.where(way == 0, spot, nc - 1 - spot)
        falling = (place + span - 1) // span
        rising = (nc - place) // span
        low = jnp.where(k < falling, falling - 1 - k, k)
        high = jnp.where(k < 4 - rising, rising + k, 3 - k)
        return jnp.where(place <= zs, low, high)

    def mate_copy(m, way, k):
        chips = pl.ds(group_at(way, k) * per, per)
        cols = pl.ds(pl.multiple_of(way * (ff // 2), 128), ff // 2)
        return remote(
            acc.at[m, chips, 1 - core, :, cols],
            mate.at[m, chips, :, cols],
            mt_send.at[m, way, k],
            mt_recv.at[m, way, k],
            buddy,
        )

    def second(k):
        def one(way, carry):
            gradient_rows(1, group_at(way, k), way * (ff // 2 // WIDE), (way + 1) * (ff // 2 // WIDE))
            for m in range(2):
                mate_copy(m, way, k).start()
            return carry

        lax.fori_loop(0, 2, one, 0)

    fetch_y = load(fc_ref, ybuf, 6)
    fetch_y.start()

    def owner_of(way, step):
        return chip_at(spot - 1 - step, nc) if way == 0 else chip_at(spot + 1 + step, nc)

    def sum_copy(m, way, sub, step, source):
        return remote(
            source,
            slots.at[m, way, sub, step],
            rs_send.at[m, way, sub, step],
            rs_recv.at[m, way, sub, step],
            ahead if way == 0 else behind,
        )

    def mate_arrivals(m, step):
        for way in range(2):
            mate_copy(m, way, step).wait_recv()

    def sum_start(m):
        for way in range(2):
            mate_copy(m, way, 0).wait_recv()
            for sub in range(SUBS):
                owner, cols = owner_of(way, 0), cols_of(way, sub)
                acc[m, owner, core, :, cols] = acc[m, owner, core, :, cols] + mate[m, owner, :, cols]
                sum_copy(m, way, sub, 0, acc.at[m, owner, core, :, cols]).start()

    def sum_step(m, step):
        @pl.when(step < 4)
        def _():
            mate_arrivals(m, step)

        for sub in range(SUBS):
            for way in range(2):
                owner, cols = owner_of(way, step), cols_of(way, sub)
                held = slots.at[m, way, sub, step - 1]
                sum_copy(m, way, sub, step - 1, held).wait_recv()
                slots[m, way, sub, step - 1] = slots[m, way, sub, step - 1] + (
                    acc[m, owner, core, :, cols] + mate[m, owner, :, cols]
                )
                sum_copy(m, way, sub, step, held).start()

    nt = ff // TILE

    def fetch(m, t, buf):
        cols = pl.ds(pl.multiple_of(t * TILE, TILE), TILE)
        return pltpu.make_async_copy(wts.at[m, :, :, :, cols], tiles.at[m, buf], tile_sem.at[m, buf])

    def put_rows(k, i, value):
        high, low = split(value)
        to = pl.ds(i * 2 * quarter, 2 * quarter)
        right[k, to, :] = high
        right[k + 1, to, :] = low

    def factor_rows(i):
        here = pl.ds(i * 2 * quarter, 2 * quarter)
        copy = load(fa_ref.at[here], sa, 0)
        copy.start()
        copy.wait()
        put_rows(0, i, sa[...])

    def opened_rows(i):
        here = pl.ds(i * 2 * quarter, 2 * quarter)
        copies = [load(uo.at[here], sx, 0), load(ru.at[here], sx2, 1)]
        for copy in copies:
            copy.start()
        for copy in copies:
            copy.wait()
        put_rows(2, i, sx[...] + sx2[...])

    def first_tile(t):
        buf = lax.rem(t, 2)
        cols = pl.ds(pl.multiple_of(t * TILE, TILE), TILE)

        @pl.when(t + 1 < nt)
        def _():
            fetch(1, t + 1, 1 - buf).start()

        fetch(1, t, buf).wait()
        weight = split(tiles[1, buf].reshape(d, TILE))
        ybuf[:, cols] = ybuf[:, cols] + product((right[0], right[1]), weight)

    def second_tile(t):
        buf = lax.rem(t, 2)
        cols = pl.ds(pl.multiple_of(t * TILE, TILE), TILE)

        @pl.when(t + 1 < nt)
        def _():
            for m in range(2):
                fetch(m, t + 1, 1 - buf).start()

        for m in range(2):
            fetch(m, t, buf).wait()
        weight = split(tiles[0, buf].reshape(d, TILE) + keep * tiles[1, buf].reshape(d, TILE))
        ybuf[:, cols] = ybuf[:, cols] + product((right[2], right[3]), weight)

    for m in range(2):

        def opening(way, carry):
            gradient_rows(1, group_at(way, 0), way * (ff // 2 // WIDE), (way + 1) * (ff // 2 // WIDE), m)
            mate_copy(m, way, 0).start()
            return carry

        lax.fori_loop(0, 2, opening, 0)
        if m == 0:
            sum_start(0)
    second(1)
    pass_on(1, steps - 1)
    late = 2 * steps - 5

    def several(tile, turn):
        def one(t, carry):
            tile(t)
            return carry

        lax.fori_loop(turn * nt // 3, (turn + 1) * nt // 3, one, 0)

    def drain_gather(step, carry):
        for m in range(2):
            for way in range(2):
                for sub in range(SUBS):
                    gather_copy(m, way, sub, step).wait_send()
        return carry

    def drain_early():
        lax.fori_loop(0, steps, drain_gather, 0)
        for m in range(2):
            for way in range(2):
                for k in range(4):
                    mate_copy(m, way, k).wait_send()
        mask_copy().wait_send()
        for side in range(2):

            @pl.when(party == side)
            def _():
                for j in range(2):
                    for copy in chunk_copies(side, j):
                        copy.wait_send()
        open_copy().wait_send()

    def forward(work):
        @pl.when(work == 3)
        def _():
            for m in range(2):
                pltpu.make_async_copy(wts.at[m, chip, core], wts.at[m, chip, core], lc_sem.at[m]).wait()
                everything = remote(wts.at[m, :, core], wts.at[m, :, 1 - core], ac_send.at[m], ac_recv.at[m], buddy)
                everything.wait_recv()
                everything.wait_send()
            fetch(1, 0, 0).start()
            fetch_y.wait()

        @pl.when(work == 4)
        def _():
            factor_rows(0)
            factor_rows(1)

        @pl.when(jnp.logical_and(work >= 5, work < 8))
        def _():
            several(first_tile, work - 5)

        @pl.when(jnp.logical_and(work > late, work <= late + 3))
        def _():
            several(second_tile, work - late - 1)

        @pl.when(work == late + 3)
        def _():
            drain_early()
            triple = load(bc_ref, got_w, 0)
            triple.start()
            triple.wait()

        @pl.when(work == late)
        def _():
            for m in range(2):
                fetch(m, 0, 0).start()
            open_copy().wait_recv()
            for i in range(2):
                opened_rows(i)

    def swap_copy(way, sub):
        cols = cols_of(way, sub)
        return remote(give.at[:, cols], got.at[:, cols], sw_send.at[way, sub], sw_recv.at[way, sub], other)

    def total(m, way, sub):
        cols = cols_of(way, sub)
        held = slots.at[m, way, sub, steps - 1]
        sum_copy(m, way, sub, steps - 1, held).wait_recv()
        return slots[m, way, sub, steps - 1] + (acc[m, chip, core, :, cols] + mate[m, chip, :, cols])

    def half_step(work, carry):
        m = lax.rem(work, 2)
        step = work // 2 + 1 - m
        forward(work)

        @pl.when(jnp.logical_and(m == 1, step < 2))
        def _():
            second(step + 2)

        @pl.when(step == 0)
        def _():
            sum_start(1)

        @pl.when(jnp.logical_and(step > 0, step < steps))
        def _():
            sum_step(m, step)

        @pl.when(step == steps)
        def _():
            for sub in range(SUBS):
                for way in range(2):
                    cols = cols_of(way, sub)
                    give[:, cols] = total(0, way, sub) - keep * got_w[:, cols]
                    swap_copy(way, sub).start()

        return carry

    lax.fori_loop(0, 2 * steps, half_step, 0)
    for sub in range(SUBS):
        for way in range(2):
            cols = cols_of(way, sub)
            dw_ref[:, cols] = total(1, way, sub) + keep * got_w[:, cols]
    for sub in range(SUBS):
        for way in range(2):
            cols = cols_of(way, sub)
            swap_copy(way, sub).wait_recv()
            dw_ref[:, cols] = dw_ref[:, cols] + got[:, cols]

    def drain(step, carry):
        for m in range(2):
            for way in range(2):
                for sub in range(SUBS):
                    sum_copy(m, way, sub, step, slots.at[m, way, sub, step]).wait_send()
        return carry

    lax.fori_loop(0, steps, drain, 0)
    for way in range(2):
        for sub in range(SUBS):
            swap_copy(way, sub).wait_send()


def body(n, x_share, w_share, g_share, fwd_a, fwd_b, fwd_c, bwd_a, bwd_b, bwd_c):
    tokens, d = x_share.shape[1:]
    rows, ff = fwd_b.shape[1:]
    nc = n // 2
    steps = nc - 1
    quarter, eighth = tokens // 4, tokens // 8
    piece = ff // (2 * SUBS)
    hbm = pl.BlockSpec(memory_space=pl.ANY)
    vmem = pl.BlockSpec(memory_space=pltpu.VMEM)
    dma = pltpu.SemaphoreType.DMA

    def shape(*dims):
        return jax.ShapeDtypeStruct(dims, F32)

    outs = pl.pallas_call(
        functools.partial(kernel, n),
        out_shape=[
            pltpu.VMEM((tokens, ff), F32),
            pltpu.VMEM((rows, ff), F32),
            shape(2, nc, 2, rows, ff),
            shape(tokens // 2, d),
            shape(tokens // 2, d),
            shape(tokens // 8, ff),
            shape(tokens, d),
            shape(tokens, d),
        ],
        in_specs=[hbm] * 9,
        out_specs=[vmem, vmem] + [hbm] * 6,
        scratch_shapes=[
            pltpu.VMEM((2, nc, 2, rows, ff), F32),
            pltpu.VMEM((2, nc, rows, ff), F32),
            pltpu.VMEM((2, 2, SUBS, steps, rows, piece), F32),
            pltpu.VMEM((3, 2, d, 2 * quarter), BF16),
            pltpu.VMEM((4, 4 * quarter, ff // 2), BF16),
            pltpu.VMEM((2 * quarter, d), F32),
            pltpu.VMEM((2 * quarter, d), F32),
            pltpu.VMEM((2 * quarter, d), F32),
            pltpu.VMEM((2 * quarter, d), F32),
            pltpu.VMEM((quarter, ff), F32),
            pltpu.VMEM((quarter, ff), F32),
            pltpu.VMEM((eighth, ff), F32),
            pltpu.VMEM((2 * quarter, d), F32),
            pltpu.VMEM((2 * quarter, d), F32),
            pltpu.VMEM((eighth, ff), F32),
            pltpu.VMEM((2, 2, nc, 2, rows, TILE), F32),
            pltpu.VMEM((rows, ff), F32),
            pltpu.VMEM((rows, ff), F32),
            pltpu.VMEM((rows, ff), F32),
            pltpu.VMEM((rows, ff), F32),
            pltpu.VMEM((rows, ff), F32),
            dma((7,)),
            dma((2, 2)),
            dma((2,)),
            dma((6,)),
            dma((6,)),
            dma((2, SUBS)),
            dma((2, SUBS)),
            dma((2, 2, SUBS, steps)),
            dma((2, 2, SUBS, steps)),
            dma((2,)),
            dma((2,)),
            dma((2, 2, SUBS, steps)),
            dma((2, 2, SUBS, steps)),
            dma((2, 2, 4)),
            dma((2, 2, 4)),
        ],
        compiler_params=pltpu.CompilerParams(collective_id=0, has_side_effects=True, vmem_limit_bytes=61_500_000),
        cost_estimate=pl.CostEstimate(flops=32 * tokens * d * ff, bytes_accessed=100 * 2**20, transcendentals=0),
    )(
        x_share[0],
        g_share[0],
        fwd_a[0],
        fwd_c[0],
        bwd_a[0],
        bwd_b[0],
        w_share[0],
        fwd_b[0],
        bwd_c[0],
    )
    return outs[0][None], outs[1][None]


def solution(mesh):
    spec = P("party", "dp", None)
    return jax.shard_map(
        functools.partial(body, mesh.shape["dp"]),
        mesh=mesh,
        in_specs=(spec,) * 9,
        out_specs=(spec, spec),
        check_vma=False,
    )
```
